128 devices in a mesh: dap: 128 (over x, y, z, core).
Axes of the slice: x: 4, y: 4, z: 4, core: 2. Of those that a mesh axis runs over, the one named last changes fastest.
Arguments:
- homolog_stack: float32 [256, 256, 256], P('dap'), may hold values from -5 to 5
- couple_tensor: float32 [256, 256, 128], P('dap'), may hold values from -6 to 6
- homolog_presence: int32 [256, 256], P('dap'), may hold values from 0 to 1
- amino_presence: int32 [256], replicated, may hold values 0 or 1
- horizontal_standard_factor: float32 [256], replicated, may hold values from 0.5 to 1.5
- horizontal_asking_matrix: bfloat16 [256, 256], replicated, may hold values from -7 to 7
- horizontal_lookup_triple: bfloat16 [256, 768], replicated, may hold values from -0.375 to 0.375
- horizontal_final_matrix: bfloat16 [256, 256], replicated, may hold values from -0.375 to 0.375
- couple_offset_factor: float32 [128], replicated, may hold values from 0.5 to 1.5
- couple_offset_matrix: bfloat16 [128, 8], replicated, may hold values from -2 to 2
- vertical_standard_factor: float32 [256], replicated, may hold values from 0.5 to 1.5
- vertical_asking_matrix: bfloat16 [256, 256], replicated, may hold values from -7 to 7
- vertical_lookup_triple: bfloat16 [256, 768], replicated, may hold values from -0.375 to 0.375
- vertical_final_matrix: bfloat16 [256, 256], replicated, may hold values from -0.375 to 0.375
- tensor_average_factor: float32 [256], replicated, may hold values from 0.5 to 1.5
- tensor_average_mapping: bfloat16 [256, 64], replicated, may hold values from -0.375 to 0.375
- tensor_average_final: bfloat16 [1024, 128], replicated, may hold values from -0.375 to 0.375
- trio_entry_factors: float32 [2, 128], replicated, may hold values from 0.5 to 1.5
- trio_flank_mappings: bfloat16 [2, 128, 512], replicated, may hold values from -0.5 to 0.5
- trio_final_switches: bfloat16 [2, 128, 128], replicated, may hold values from -0.5 to 0.5
- trio_multiplied_factors: float32 [2, 128], replicated, may hold values from 0.5 to 1.5
- trio_final_matrices: bfloat16 [2, 128, 128], replicated, may hold values from -1 to 1
Outputs:
- msa_out: float32 [256, 256, 256], P(None, 'dap')
- pair_out: float32 [256, 256, 128], P('dap')
The draws below stay inside these ranges and needn't reach their ends.
All inputs are finite; a program needn't handle non-finite values.
Results may differ from the reference program's by a relative error of at most 0.015.
Values may be sent and summed in bfloat16 or wider, within the bound.
A program may use at most 64 MiB of HBM per device.

```python
import math
import jax
import jax.numpy as jnp
from jax import lax

ALIGNED_FEATURES = 256
CZ = 128
FOCUS_NUMBER = 8
PER_FOCUS_WIDTH = 32
TENSOR_HIDDEN = 32
TRI_HID = 128
CHAIN_WINDOW = 256
ALIGNED_STRANDS = 256


def draw_homolog_presence(key, part):
    leading_lookup, second_key, third_key = jax.random.split(jax.random.fold_in(key, 11), 3)
    column_rate = jax.random.randint(third_key, (1, CHAIN_WINDOW), 15, 101)
    existing_flag = jax.random.randint(leading_lookup, (ALIGNED_STRANDS, CHAIN_WINDOW), 0, 100) < column_rate
    column_alive = jax.random.randint(second_key, (1, CHAIN_WINDOW), 0, 100) < 97
    return jnp.logical_and(existing_flag, column_alive).astype(jnp.int32)


def draw_homolog_stack(key, part):
    profile_key, noise_key = jax.random.split(jax.random.fold_in(key, 53))
    profile = jnp.clip(jax.random.normal(profile_key, (1, CHAIN_WINDOW, ALIGNED_FEATURES), jnp.float32), -3.0, 3.0)
    noise = 0.6 * jnp.clip(jax.random.normal(noise_key, (ALIGNED_STRANDS, CHAIN_WINDOW, ALIGNED_FEATURES), jnp.float32), -3.0, 3.0)
    return profile + noise


def query_weights(key):
    content_vectors = jnp.clip(jax.random.normal(key, (ALIGNED_FEATURES, FOCUS_NUMBER * PER_FOCUS_WIDTH), jnp.float32) * (2.0 / math.sqrt(ALIGNED_FEATURES)), -7.0, 7.0)
    return content_vectors


def draw_horizontal_asking_matrix(key, part):
    return query_weights(jax.random.fold_in(key, 21)).astype(jnp.bfloat16)


def draw_vertical_asking_matrix(key, part):
    return query_weights(jax.random.fold_in(key, 37)).astype(jnp.bfloat16)


def touch_ends(drawn, key, smallest, largest):
    longest = drawn.shape.index(max(drawn.shape))
    spots = []
    for shift in (0, 1):
        where = [jax.random.randint(jax.random.fold_in(key, axis), (), 0, length) for axis, length in enumerate(drawn.shape)]
        where[longest] = (where[longest] + shift) % drawn.shape[longest]
        spots.append(tuple(where))
    return drawn.at[spots[0]].set(smallest).at[spots[1]].set(largest)


def level_of(own_key, shape, cuts, smallest, largest):
    level, own = 1.0, jax.random.fold_in(own_key, 6)
    for axis_at, shards_of in cuts:
        draws = jnp.exp(jax.random.uniform(jax.random.fold_in(own, axis_at), (shards_of,), jnp.float32, smallest / len(cuts), largest / len(cuts)))
        level = level * jnp.repeat(draws, shape[axis_at] // shards_of).reshape([-1 if axis == axis_at else 1 for axis in range(len(shape))])
    return level


def bell_draw(rng, shape, deviation, limit, pieces=(), dtype=jnp.bfloat16):
    factor_of = level_of(rng, shape, pieces, -0.22, 0.18) if pieces else 1.0
    values = jax.random.normal(rng, shape, jnp.float32) * deviation * factor_of
    return jnp.minimum(jnp.maximum(values, -limit), limit).astype(dtype)


def setup_inputs(seed: int = 0) -> dict:
    streams_of = jax.random.split(jax.random.key(seed), 23)
    return {
        "homolog_stack": draw_homolog_stack(jax.random.fold_in(streams_of[22], 71), 0),
        "couple_tensor": bell_draw(streams_of[1], (CHAIN_WINDOW, CHAIN_WINDOW, CZ), 1.0, 6.0, ((0, 128),), jnp.float32),
        "homolog_presence": draw_homolog_presence(jax.random.fold_in(streams_of[22], 71), 0),
        "amino_presence": touch_ends((jax.random.randint(streams_of[3], (CHAIN_WINDOW,), 0, 10) < 9).astype(jnp.int32), jax.random.fold_in(streams_of[3], 1), 0, 1),
        "horizontal_standard_factor": jnp.clip(jax.random.uniform(streams_of[4], (ALIGNED_FEATURES,), jnp.float32, 0.5, 1.5), 0.5, 1.5),
        "horizontal_asking_matrix": draw_horizontal_asking_matrix(jax.random.fold_in(streams_of[22], 71), 0),
        "horizontal_lookup_triple": bell_draw(streams_of[6], (ALIGNED_FEATURES, 3 * FOCUS_NUMBER * PER_FOCUS_WIDTH), ALIGNED_FEATURES ** -0.5, 0.375),
        "horizontal_final_matrix": bell_draw(streams_of[7], (FOCUS_NUMBER * PER_FOCUS_WIDTH, ALIGNED_FEATURES), (FOCUS_NUMBER * PER_FOCUS_WIDTH) ** -0.5, 0.375),
        "couple_offset_factor": jnp.clip(jax.random.uniform(streams_of[8], (CZ,), jnp.float32, 0.5, 1.5), 0.5, 1.5),
        "couple_offset_matrix": bell_draw(streams_of[9], (CZ, FOCUS_NUMBER), (CZ // 16) ** -0.5, 2.0),
        "vertical_standard_factor": jnp.clip(jax.random.uniform(streams_of[10], (ALIGNED_FEATURES,), jnp.float32, 0.5, 1.5), 0.5, 1.5),
        "vertical_asking_matrix": draw_vertical_asking_matrix(jax.random.fold_in(streams_of[22], 71), 0),
        "vertical_lookup_triple": bell_draw(streams_of[12], (ALIGNED_FEATURES, 3 * FOCUS_NUMBER * PER_FOCUS_WIDTH), ALIGNED_FEATURES ** -0.5, 0.375),
        "vertical_final_matrix": bell_draw(streams_of[13], (FOCUS_NUMBER * PER_FOCUS_WIDTH, ALIGNED_FEATURES), (FOCUS_NUMBER * PER_FOCUS_WIDTH) ** -0.5, 0.375),
        "tensor_average_factor": jnp.clip(jax.random.uniform(streams_of[14], (ALIGNED_FEATURES,), jnp.float32, 0.5, 1.5), 0.5, 1.5),
        "tensor_average_mapping": bell_draw(streams_of[15], (ALIGNED_FEATURES, 2 * TENSOR_HIDDEN), ALIGNED_FEATURES ** -0.5, 0.375),
        "tensor_average_final": bell_draw(streams_of[16], (TENSOR_HIDDEN * TENSOR_HIDDEN, CZ), (TENSOR_HIDDEN * TENSOR_HIDDEN // 4) ** -0.5, 0.375),
        "trio_entry_factors": jnp.clip(jax.random.uniform(streams_of[17], (2, CZ), jnp.float32, 0.5, 1.5), 0.5, 1.5),
        "trio_flank_mappings": bell_draw(streams_of[18], (2, CZ, 4 * TRI_HID), CZ ** -0.5, 0.5),
        "trio_final_switches": bell_draw(streams_of[19], (2, CZ, CZ), CZ ** -0.5, 0.5),
        "trio_multiplied_factors": jnp.clip(jax.random.uniform(streams_of[20], (2, TRI_HID), jnp.float32, 0.5, 1.5), 0.5, 1.5),
        "trio_final_matrices": bell_draw(streams_of[21], (2, TRI_HID, CZ), (TRI_HID // 4) ** -0.5, 1.0),
    }


EPSILON = 1e-05
MASK_PENALTY_SCALE = 1000000000.0

def standardize_features(content_vectors, gain, axis):
    centred = content_vectors - lax.optimization_barrier(jnp.mean(content_vectors, axis=axis, keepdims=True))
    spread = lax.optimization_barrier(jnp.mean(centred * centred, axis=axis, keepdims=True))
    return centred * lax.rsqrt(spread + EPSILON) * gain

def triangle(pair_now, gain_in, proj_weight, gate_weight, gain_mid, final_weight, res_float, incoming):
    hidden = TRI_HID
    standardized_source = standardize_features(pair_now, gain_in.astype(jnp.float32), -1).astype(jnp.bfloat16)
    projected = jnp.dot(standardized_source, proj_weight, preferred_element_type=jnp.float32)
    pair_mask = (res_float[:, None] * res_float[None, :])[..., None]
    left_side = (jax.nn.sigmoid(projected[..., hidden:2 * hidden]) * projected[..., :hidden] * pair_mask).astype(jnp.bfloat16)
    right_side = (jax.nn.sigmoid(projected[..., 3 * hidden:]) * projected[..., 2 * hidden:3 * hidden] * pair_mask).astype(jnp.bfloat16)
    gating = jax.nn.sigmoid(jnp.dot(standardized_source, gate_weight, preferred_element_type=jnp.float32))
    if incoming:
        product = jnp.einsum('kic,kjc->ijc', left_side.astype(jnp.float32), right_side.astype(jnp.float32))
    else:
        product = jnp.einsum('ikc,jkc->ijc', left_side.astype(jnp.float32), right_side.astype(jnp.float32))
    product = product.astype(jnp.bfloat16)
    product_normed = standardize_features(product.astype(jnp.float32), gain_mid.astype(jnp.float32), -1).astype(jnp.bfloat16)
    return pair_now + jnp.dot(product_normed, final_weight, preferred_element_type=jnp.float32) * gating

def reference(homolog_stack, couple_tensor, homolog_presence, amino_presence, horizontal_standard_factor, horizontal_asking_matrix, horizontal_lookup_triple, horizontal_final_matrix, couple_offset_factor, couple_offset_matrix, vertical_standard_factor, vertical_asking_matrix, vertical_lookup_triple, vertical_final_matrix, tensor_average_factor, tensor_average_mapping, tensor_average_final, trio_entry_factors, trio_flank_mappings, trio_final_switches, trio_multiplied_factors, trio_final_matrices):
    nested_function = FOCUS_NUMBER * PER_FOCUS_WIDTH
    scaling = 1.0 / math.sqrt(PER_FOCUS_WIDTH)
    mask_as_float = homolog_presence.astype(jnp.float32)
    mask_penalty = MASK_PENALTY_SCALE * (mask_as_float - 1.0)
    standardized_source = standardize_features(homolog_stack, horizontal_standard_factor.astype(jnp.float32), -1).astype(jnp.bfloat16)
    queries = (jnp.dot(standardized_source, horizontal_asking_matrix, preferred_element_type=jnp.float32) * scaling).astype(jnp.bfloat16)
    others = jnp.dot(standardized_source, horizontal_lookup_triple, preferred_element_type=jnp.float32)
    keys_all = others[..., :nested_function].astype(jnp.bfloat16)
    content_entire = others[..., nested_function:2 * nested_function].astype(jnp.bfloat16)
    sigmoid_switches = jax.nn.sigmoid(others[..., 2 * nested_function:])
    pair_normed = standardize_features(couple_tensor, couple_offset_factor.astype(jnp.float32), -1).astype(jnp.bfloat16)
    pair_bias = jnp.dot(pair_normed, couple_offset_matrix, preferred_element_type=jnp.float32).astype(jnp.bfloat16)
    bias_heads = jnp.transpose(pair_bias, (2, 0, 1)).astype(jnp.float32)

    def row_attend(items):
        query_seq, key_seq, value_seq, penalty_seq = items
        shaped = (CHAIN_WINDOW, FOCUS_NUMBER, PER_FOCUS_WIDTH)
        scores = jnp.einsum('ihc,jhc->hij', query_seq.reshape(shaped).astype(jnp.float32), key_seq.reshape(shaped).astype(jnp.float32))
        scores = scores + bias_heads + penalty_seq[None, None, :]
        softmax_probabilities = jax.nn.softmax(scores, axis=-1).astype(jnp.bfloat16)
        mixed = jnp.einsum('hij,jhc->ihc', softmax_probabilities.astype(jnp.float32), value_seq.reshape(shaped).astype(jnp.float32))
        return mixed.reshape(CHAIN_WINDOW, nested_function)
    focused_content = lax.map(row_attend, (queries, keys_all, content_entire, mask_penalty))
    homolog_stack_horizontal = homolog_stack + jnp.dot((focused_content * sigmoid_switches).astype(jnp.bfloat16), horizontal_final_matrix, preferred_element_type=jnp.float32)
    reformed4 = (ALIGNED_STRANDS, CHAIN_WINDOW, FOCUS_NUMBER, PER_FOCUS_WIDTH)
    standardized_source = standardize_features(homolog_stack_horizontal, vertical_standard_factor.astype(jnp.float32), -1).astype(jnp.bfloat16)
    queries = (jnp.dot(standardized_source, vertical_asking_matrix, preferred_element_type=jnp.float32) * scaling).astype(jnp.bfloat16).reshape(reformed4)
    others = jnp.dot(standardized_source, vertical_lookup_triple, preferred_element_type=jnp.float32)
    keys_all = others[..., :nested_function].astype(jnp.bfloat16).reshape(reformed4)
    content_entire = others[..., nested_function:2 * nested_function].astype(jnp.bfloat16).reshape(reformed4)
    sigmoid_switches = jax.nn.sigmoid(others[..., 2 * nested_function:])
    scores = jnp.einsum('sihc,tihc->ihst', queries.astype(jnp.float32), keys_all.astype(jnp.float32))
    scores = scores + jnp.transpose(mask_penalty)[:, None, None, :]
    softmax_probabilities = jax.nn.softmax(scores, axis=-1).astype(jnp.bfloat16)
    focused_content = jnp.einsum('uovg,guox->vuox', softmax_probabilities.astype(jnp.float32), content_entire.astype(jnp.float32)).reshape(ALIGNED_STRANDS, CHAIN_WINDOW, nested_function)
    alignment_after_columns = homolog_stack_horizontal + jnp.dot((focused_content * sigmoid_switches).astype(jnp.bfloat16), vertical_final_matrix, preferred_element_type=jnp.float32)
    standardized_source = standardize_features(alignment_after_columns, tensor_average_factor.astype(jnp.float32), -1).astype(jnp.bfloat16)
    halves = jnp.dot(standardized_source, tensor_average_mapping, preferred_element_type=jnp.float32)
    left_proj = (halves[..., :TENSOR_HIDDEN] * mask_as_float[..., None]).astype(jnp.bfloat16)
    right_proj = (halves[..., TENSOR_HIDDEN:] * mask_as_float[..., None]).astype(jnp.bfloat16)
    right_float = right_proj.astype(jnp.float32)

    def opm_row(items):
        left_row, mask_row = items
        outer = jnp.einsum('sa,sjb->jab', left_row.astype(jnp.float32), right_float)
        outer = outer.astype(jnp.bfloat16).reshape(CHAIN_WINDOW, TENSOR_HIDDEN * TENSOR_HIDDEN)
        counts = jnp.dot(mask_row, mask_as_float, precision=lax.Precision.HIGHEST)
        return jnp.dot(outer, tensor_average_final, preferred_element_type=jnp.float32) / jnp.maximum(counts, 1.0)[:, None]
    product = lax.map(opm_row, (jnp.moveaxis(left_proj, 1, 0), jnp.transpose(mask_as_float)))
    pair_one = couple_tensor + product
    res_float = amino_presence.astype(jnp.float32)
    pair_two = triangle(pair_one, trio_entry_factors[0], trio_flank_mappings[0], trio_final_switches[0], trio_multiplied_factors[0], trio_final_matrices[0], res_float, False)
    pair_after_incoming = triangle(pair_two, trio_entry_factors[1], trio_flank_mappings[1], trio_final_switches[1], trio_multiplied_factors[1], trio_final_matrices[1], res_float, True)
    return (alignment_after_columns, pair_after_incoming)
```

```python
import math

import jax
import jax.numpy as jnp
from jax import lax
from jax.experimental import pallas as pl
from jax.experimental.pallas import tpu as pltpu
from jax.sharding import PartitionSpec as P

N = 128
S = 256
H = 256
CZ = 128
HEADS = 8
WIDTH = 32
PLANE = 16
LINE = 8
BR = 40
EPS = 1e-05
PENALTY = 1e9
SCALE = 1.0 / math.sqrt(WIDTH)
F32, BF16 = jnp.float32, jnp.bfloat16
MESH = pl.DeviceIdType.MESH


def dot(a, b):
    return jnp.dot(a, b, preferred_element_type=F32)


def dot_nt(a, b):
    return lax.dot_general(a, b, (((1,), (1,)), ((), ())), preferred_element_type=F32)


def norm(x, gain, axis=-1):
    centred = x - jnp.mean(x, axis=axis, keepdims=True)
    spread = jnp.mean(centred * centred, axis=axis, keepdims=True)
    return centred * lax.rsqrt(spread + EPS) * gain


def send(src, dst, ssem, rsem, to):
    pltpu.make_async_remote_copy(
        src_ref=src, dst_ref=dst, send_sem=ssem, recv_sem=rsem, device_id=(to,), device_id_type=MESH
    ).start()


def landed(like, sem):
    pltpu.make_async_copy(like, like, sem).wait()


def every_other(halves, first):
    return jnp.concatenate([halves[c, pl.ds(first, 128, stride=2), :] for c in range(2)], axis=1)


def attend(q, k, v, o, bias, pens, heads_lane):
    o[...] = jnp.zeros_like(o)

    def head(h, _):
        sel = jnp.logical_and(heads_lane >= h * WIDTH, heads_lane < (h + 1) * WIDTH)
        only = sel.astype(F32).astype(BF16)
        for t in range(2):
            vm = v[t] * only
            for r in range(2):
                rows = slice(r * 128, (r + 1) * 128)
                scores = dot_nt(q[t, rows] * only, k[t])
                if bias is not None:
                    scores = scores + bias(h, r)
                scores = scores + pens[t]
                top = jnp.max(scores, axis=-1, keepdims=True)
                e = jnp.exp(scores - top)
                p = (e * (1.0 / jnp.sum(e, axis=-1, keepdims=True))).astype(BF16)
                o[t, rows] += dot(p, vm)
        return 0

    lax.fori_loop(0, HEADS, head, 0)


def body(
    msa, pair, pres, amino, g_row, wq1, wkvg1, wo1, g_bias, wb,
    g_col, wq2, wkvg2, wo2, g_opm, wlr, wfin, g_in, wproj, wgate, g_mid, wout,
    msa_out, pair_out,
    bsend, bg, b32, xn, msah, q, k, v, gate, o, a32, asend, arecv, xc, pm, pmt, cnt,
    lsend, rsend, lg, rg, r32, rp, lhs2, bd, osend, og, wt, wlrt, gmt, pad,
    t32, tsend, trecv, tgate, p32, psend, precv, pnow,
    ssem, rsem,
):
    me = lax.axis_index("dap")
    core = lax.rem(me, 2)
    partner = me + 1 - 2 * core
    chip = me // 2
    my_u, my_v = me // LINE, lax.rem(me, LINE)

    barrier = pltpu.get_barrier_semaphore()

    def hello(i, _):
        pl.semaphore_signal(
            barrier, inc=1, device_id=(lax.rem(me + i, N),), device_id_type=MESH
        )
        return 0

    lax.fori_loop(1, N, hello, 0)

    pad[...] = jnp.zeros_like(pad)
    pad[0:CZ, 0:HEADS] = wb[...].astype(F32)
    wbt = pad[0:CZ, :].T.astype(BF16)[0:16]
    for r in range(2):
        pn = norm(pair[r], g_bias[...][None, :]).astype(BF16)
        bt = dot_nt(wbt, pn)
        for j in range(2):
            at = (r * 2 + j) * 8
            bsend[at : at + 8, :] = bt[0:8, j * 128 : (j + 1) * 128].astype(BF16)
    pad[0:8, :] = jnp.zeros((8, 128), F32)
    presence = pres[...].astype(F32)
    for r in range(2):
        for j in range(2):
            pad[r * 2 + j : r * 2 + j + 1, :] = presence[r : r + 1, j * 128 : (j + 1) * 128]
    bsend[32:40, :] = pad[0:8, :].astype(BF16)
    bg[core, chip] = bsend[...]

    pl.semaphore_wait(barrier, N - 1)

    def spread_bias(i, _):
        to = lax.rem(me + 2 * i, N)
        send(bsend, bg.at[core, chip], ssem.at[0], rsem.at[0], to)
        return 0

    lax.fori_loop(1, N // 2, spread_bias, 0)

    lanes = lax.broadcasted_iota(jnp.int32, (1, H), 1)
    for s in range(2):
        x = norm(msa[s], g_row[...][None, :])
        for c in range(2):
            xn[c] = x[:, c * 128 : (c + 1) * 128]
            msah[s, c] = msa[s, :, c * 128 : (c + 1) * 128]
        xb = x.astype(BF16)
        k[s] = dot(xb, wkvg1[:, 0:H]).astype(BF16)
        v[s] = dot(xb, wkvg1[:, H : 2 * H]).astype(BF16)
        for r in range(2):
            rows = slice(r * 128, (r + 1) * 128)
            xr = every_other(xn, r).astype(BF16)
            q[s, rows] = (dot(xr, wq1[...]) * SCALE).astype(BF16)
            gate[s, rows] = jax.nn.sigmoid(dot(xr, wkvg1[:, 2 * H :]))

    for w in range(2):
        for c in range(4):
            cols = slice(c * 128, (c + 1) * 128)
            wt[w, cols, :] = wproj[w, :, cols].astype(F32).T.astype(BF16)
        gmt[w] = jnp.broadcast_to(g_mid[w : w + 1, :], (CZ, CZ)).T
    pad[:, 0:64] = wlr[...].astype(F32)
    wlrt[...] = pad[...].T.astype(BF16)[0:64]
    p32[...] = wfin[0:512, :].astype(F32)
    t32[0:512, :] = wfin[512:1024, :].astype(F32)
    bd[...] = jnp.zeros_like(bd)
    for b in range(32):
        part = jnp.concatenate(
            [p32[pl.ds(b, 16, stride=32), :], t32[pl.ds(b, 16, stride=32), :]], axis=0
        ).astype(BF16)
        for i in range(4):
            bd[b * 128 + i * 32 : b * 128 + (i + 1) * 32, i * 128 : (i + 1) * 128] = part

    landed(bg.at[0, pl.ds(0, N // 2 - 1)], rsem.at[0])
    send(bg.at[core], bg.at[core], ssem.at[1], rsem.at[1], partner)
    landed(bg.at[0], rsem.at[1])

    def widen(d, _):
        b32[pl.ds(pl.multiple_of(d * BR, 8), BR), :] = bg[lax.rem(d, 2), d // 2].astype(F32)
        return 0

    lax.fori_loop(0, N, widen, 0)

    def bias(h, r):
        return jnp.concatenate(
            [b32[pl.ds((r * 2 + j) * 8 + h, 128, stride=BR), :] for j in range(2)], axis=1
        )

    pens = [PENALTY * (presence[s : s + 1, :] - 1.0) for s in range(2)]
    attend(q, k, v, o, bias, pens, lanes)

    for s in range(2):
        for r in range(2):
            rows = slice(r * 128, (r + 1) * 128)
            y = (o[s, rows] * gate[s, rows]).astype(BF16)
            one = every_other(msah.at[s], r) + dot(y, wo1[...])
            for c in range(2):
                a32[pl.ds((s * 2 + r) * 2 + c, 128, stride=8), :] = one[:, c * 128 : (c + 1) * 128]
    asend[...] = a32[...].reshape(N, 8, 128).astype(BF16)
    arecv[me] = asend[me]

    def exchange(src, dst, sem):
        def one(i, _):
            to = lax.rem(me + i, N)
            send(src.at[to], dst.at[me], ssem.at[sem], rsem.at[sem], to)
            return 0

        lax.fori_loop(1, N, one, 0)

    def received(src, dst, sem):
        landed(dst.at[pl.ds(0, N - 1)], rsem.at[sem])
        landed(src.at[pl.ds(0, N - 1)], ssem.at[sem])

    exchange(asend, arecv, 2)

    for s in range(2):
        for j in range(2):
            pm[s * 128 : (s + 1) * 128, j * 128 : (j + 1) * 128] = b32[
                pl.ds(32 + s * 2 + j, 128, stride=BR), :
            ]
    pmt[...] = pm[...].T.astype(BF16)
    own = lax.broadcasted_iota(jnp.int32, (16, S), 0) + 2 * me
    hot = (lax.broadcasted_iota(jnp.int32, (16, S), 1) == own).astype(F32).astype(BF16)
    mine = dot(hot, pmt[...])
    pmb = pm[...].astype(BF16)
    for r in range(2):
        hot_c = (lax.broadcasted_iota(jnp.int32, (S, 128), 0) == 2 * me + r).astype(F32)
        col = dot(pmb, hot_c.astype(BF16)).astype(BF16)
        cnt[r] = 1.0 / jnp.maximum(dot(pmt[...], col), 1.0)

    received(asend, arecv, 2)
    a32[...] = arecv[...].astype(F32).reshape(N * 8, 128)
    for r in range(2):
        for s in range(2):
            for c in range(2):
                xc[r, s * 128 : (s + 1) * 128, c * 128 : (c + 1) * 128] = a32[
                    pl.ds((s * 2 + r) * 2 + c, 128, stride=8), :
                ]
        xb = norm(xc[r], g_col[...][None, :]).astype(BF16)
        q[r] = (dot(xb, wq2[...]) * SCALE).astype(BF16)
        k[r] = dot(xb, wkvg2[:, 0:H]).astype(BF16)
        v[r] = dot(xb, wkvg2[:, H : 2 * H]).astype(BF16)
        gate[r] = jax.nn.sigmoid(dot(xb, wkvg2[:, 2 * H :]))
    pens = [PENALTY * (mine[r : r + 1, :] - 1.0) for r in range(2)]
    attend(q, k, v, o, None, pens, lanes)
    for r in range(2):
        y = (o[r] * gate[r]).astype(BF16)
        done = xc[r] + dot(y, wo2[...])
        for s in range(2):
            for c in range(2):
                msa_out[pl.ds(s * 4 + c * 2 + r, 128, stride=8), :] = done[
                    s * 128 : (s + 1) * 128, c * 128 : (c + 1) * 128
                ]
        xb = norm(done, g_opm[...][None, :]).astype(BF16)
        halves = dot_nt(wlrt[...], xb) * mine[r : r + 1, :]
        lsend[r * 32 : (r + 1) * 32, :] = halves[0:32].astype(BF16)
        rsend[r * 32 : (r + 1) * 32, :] = halves[32:64].astype(BF16)

    lg[my_u] = lsend[...]
    rg[my_v] = rsend[...]

    def spread_left(i, _):
        send(lsend, lg.at[my_u], ssem.at[3], rsem.at[3], lax.rem(me + LINE * i, N))
        return 0

    def spread_right(i, _):
        to = my_u * LINE + lax.rem(my_v + i, LINE)
        send(rsend, rg.at[my_v], ssem.at[4], rsem.at[4], to)
        return 0

    lax.fori_loop(1, PLANE, spread_left, 0)
    lax.fori_loop(1, LINE, spread_right, 0)
    landed(rg.at[pl.ds(0, LINE - 1)], rsem.at[4])
    for c in range(2):
        r32[c] = rg[:, :, c * 128 : (c + 1) * 128].astype(F32).reshape(512, 128)
    for b in range(32):
        rp[b * 16 : (b + 1) * 16, :] = jnp.concatenate(
            [r32[c, pl.ds(b, 16, stride=32), :] for c in range(2)], axis=1
        ).astype(BF16)
    landed(lg.at[pl.ds(0, PLANE - 1)], rsem.at[3])
    for g in range(8):
        lb = lg[2 * g : 2 * g + 2].reshape(128, S)
        u = dot_nt(rp[...], lb).astype(BF16)
        for b in range(32):
            lhs2[g * 16 : (g + 1) * 16, b * 128 : (b + 1) * 128] = u[b * 16 : (b + 1) * 16]
    block = dot(lhs2[...], bd[...])
    for u in range(PLANE):
        for r in range(2):
            at = 2 * (u % 2) + r
            osend[u, r] = block[
                (u // 2) * 16 : (u // 2 + 1) * 16, at * 128 : (at + 1) * 128
            ].astype(BF16)
    og[my_u] = osend[my_u]

    def give_back(i, _):
        to_u = lax.rem(my_u + i, PLANE)
        send(osend.at[to_u], og.at[my_u], ssem.at[5], rsem.at[5], to_u * LINE + my_v)
        return 0

    lax.fori_loop(1, PLANE, give_back, 0)
    landed(og.at[pl.ds(0, PLANE - 1)], rsem.at[5])
    for r in range(2):
        delta = og[:, r].astype(F32).reshape(S, CZ)
        pnow[r] = pair[r] + delta * cnt[r]

    am = amino[...].astype(F32)[None, :]
    for w in range(2):
        for r in range(2):
            x = norm(pnow[r], g_in[w : w + 1, :]).astype(BF16)
            here = jnp.sum(jnp.where(lanes == 2 * me + r, am, 0.0), axis=-1, keepdims=True)
            mask = am * here
            pt = dot_nt(wt[w], x)
            for side in range(2):
                at = side * 256
                val = jax.nn.sigmoid(pt[at + 128 : at + 256]) * pt[at : at + 128] * mask
                for j in range(2):
                    t32[pl.ds(side * 4 + r * 2 + j, 128, stride=8), :] = val[
                        :, j * 128 : (j + 1) * 128
                    ]
            tgate[r] = jax.nn.sigmoid(dot(x, wgate[w]))
        tsend[w] = t32[...].reshape(N, 8, 128).astype(BF16)
        trecv[w, me] = tsend[w, me]
        exchange(tsend.at[w], trecv.at[w], 6 + 2 * w)
        received(tsend.at[w], trecv.at[w], 6 + 2 * w)
        t32[...] = trecv[w].astype(F32).reshape(N * 8, 128)
        sides = []
        for side in range(2):
            sides.append(
                jnp.concatenate(
                    [
                        jnp.concatenate(
                            [
                                t32[pl.ds(side * 4 + r * 2 + j, 128, stride=8), :]
                                for j in range(2)
                            ],
                            axis=1,
                        )
                        for r in range(2)
                    ],
                    axis=0,
                )
            )
        if w == 0:
            prod = dot_nt(sides[0].astype(BF16), sides[1].astype(BF16))
        else:
            prod = dot(sides[0].T.astype(BF16), sides[1].astype(BF16))
        for j in range(2):
            xn[j] = prod[:, j * 128 : (j + 1) * 128]
        for r in range(2):
            for j in range(2):
                rows = pl.ds(r * 128, 128) if w == 0 else pl.ds(r, 128, stride=2)
                p32[pl.ds(r * 2 + j, 128, stride=4), :] = xn[j, rows, :]
        psend[w] = p32[...].reshape(N, 4, 128).astype(BF16)
        precv[w, me] = psend[w, me]
        exchange(psend.at[w], precv.at[w], 7 + 2 * w)
        received(psend.at[w], precv.at[w], 7 + 2 * w)
        p32[...] = precv[w].astype(F32).reshape(N * 4, 128)
        for r in range(2):
            for j in range(2):
                pn = norm(p32[pl.ds(r * 2 + j, 128, stride=4), :], gmt[w], axis=0)
                update = dot(pn.T.astype(BF16), wout[w])
                rows = pl.ds(j, 128, stride=2) if w == 0 else pl.ds(j * 128, 128)
                new = pnow[r, rows, :] + update * tgate[r, rows, :]
                if w == 0:
                    pnow[r, rows, :] = new
                else:
                    pair_out[r, rows, :] = new

    landed(bg.at[0, pl.ds(0, N // 2 - 1)], ssem.at[0])
    landed(bg.at[0], ssem.at[1])
    landed(lg.at[pl.ds(0, PLANE - 1)], ssem.at[3])
    landed(rg.at[pl.ds(0, LINE - 1)], ssem.at[4])
    landed(og.at[pl.ds(0, PLANE - 1)], ssem.at[5])


SCRATCH = [
    ((BR, 128), BF16),
    ((2, N // 2, BR, 128), BF16),
    ((N * BR, 128), F32),
    ((2, S, 128), F32),
    ((2, 2, S, 128), F32),
    ((2, S, H), BF16),
    ((2, S, H), BF16),
    ((2, S, H), BF16),
    ((2, S, H), F32),
    ((2, S, H), F32),
    ((N * 8, 128), F32),
    ((N, 8, 128), BF16),
    ((N, 8, 128), BF16),
    ((2, S, H), F32),
    ((S, S), F32),
    ((S, S), BF16),
    ((2, S, CZ), F32),
    ((64, S), BF16),
    ((64, S), BF16),
    ((PLANE, 64, S), BF16),
    ((LINE, 64, S), BF16),
    ((2, 512, 128), F32),
    ((512, S), BF16),
    ((128, 4096), BF16),
    ((4096, 512), BF16),
    ((PLANE, 2, 16, 128), BF16),
    ((PLANE, 2, 16, 128), BF16),
    ((2, 512, 128), BF16),
    ((64, H), BF16),
    ((2, CZ, CZ), F32),
    ((H, 128), F32),
    ((N * 8, 128), F32),
    ((2, N, 8, 128), BF16),
    ((2, N, 8, 128), BF16),
    ((2, S, CZ), F32),
    ((N * 4, 128), F32),
    ((2, N, 4, 128), BF16),
    ((2, N, 4, 128), BF16),
    ((2, S, CZ), F32),
]


def shards(*args):
    vmem = pl.BlockSpec(memory_space=pltpu.VMEM)
    flat, pair = pl.pallas_call(
        body,
        out_shape=(
            jax.ShapeDtypeStruct((S * 4, 128), F32),
            jax.ShapeDtypeStruct((2, S, CZ), F32),
        ),
        in_specs=[vmem] * len(args),
        out_specs=(vmem, vmem),
        scratch_shapes=[pltpu.VMEM(shape, dtype) for shape, dtype in SCRATCH]
        + [pltpu.SemaphoreType.DMA((10,)), pltpu.SemaphoreType.DMA((10,))],
        compiler_params=pltpu.CompilerParams(
            collective_id=0, has_side_effects=True, vmem_limit_bytes=60 << 20
        ),
    )(*args)
    return flat.reshape(S, 2, 2, 128).transpose(0, 2, 1, 3).reshape(S, 2, H), pair


def solution(mesh):
    rows = P("dap", None, None)
    return jax.shard_map(
        shards,
        mesh=mesh,
        in_specs=(rows, rows, P("dap", None)) + (P(),) * 19,
        out_specs=(P(None, "dap", None), rows),
        check_vma=False,
    )
```

```python
import math

import jax
import jax.numpy as jnp
from jax import lax
from jax.experimental import pallas as pl
from jax.experimental.pallas import tpu as pltpu
from jax.sharding import PartitionSpec as P

N = 128
S = 256
H = 256
CZ = 128
HEADS = 8
WIDTH = 32
PLANE = 16
LINE = 8
BA, BB = 24, 16
HOPS = (0, 1, 2, 1)
FAR_FIRST = sorted(
    [(a, b, c) for a in range(4) for b in range(4) for c in range(4)],
    key=lambda o: -(HOPS[o[0]] + HOPS[o[1]] + HOPS[o[2]]),
)
EPS = 1e-05
PENALTY = 1e9
SCALE = 1.0 / math.sqrt(WIDTH)
F32, BF16 = jnp.float32, jnp.bfloat16
MESH = pl.DeviceIdType.MESH


def dot(a, b):
    return jnp.dot(a, b, preferred_element_type=F32)


def dot_nt(a, b):
    return lax.dot_general(a, b, (((1,), (1,)), ((), ())), preferred_element_type=F32)


def norm(x, gain, axis=-1):
    centred = x - jnp.mean(x, axis=axis, keepdims=True)
    spread = jnp.mean(centred * centred, axis=axis, keepdims=True)
    return centred * lax.rsqrt(spread + EPS) * gain


def send(src, dst, ssem, rsem, to):
    pltpu.make_async_remote_copy(
        src_ref=src, dst_ref=dst, send_sem=ssem, recv_sem=rsem, device_id=(to,), device_id_type=MESH
    ).start()


def landed(like, sem):
    pltpu.make_async_copy(like, like, sem).wait()


def every_other(halves, first):
    return jnp.concatenate([halves[c, pl.ds(first, 128, stride=2), :] for c in range(2)], axis=1)


def head_lanes(h):
    lanes = lax.broadcasted_iota(jnp.int32, (1, H), 1)
    return jnp.logical_and(lanes >= h * WIDTH, lanes < (h + 1) * WIDTH).astype(F32).astype(BF16)


def spread_heads(v, vbd, t):
    for h in range(HEADS):
        vbd[t, h * S : (h + 1) * S, :] = v * head_lanes(h)


def attend_head(h, q, kt, prob, bias, pens):
    only = head_lanes(h)
    for t in range(2):
        scores = dot(q[t] * only, kt[t])
        if bias is not None:
            scores = scores + bias
        scores = scores + pens[t]
        top = jnp.max(scores, axis=-1, keepdims=True)
        e = jnp.exp(scores - top)
        prob[t, :, h * S : (h + 1) * S] = (
            e * (1.0 / jnp.sum(e, axis=-1, keepdims=True))
        ).astype(BF16)


def body(
    msa, pair, pres, amino, g_row, wq1, wkvg1, wo1, g_bias, wb,
    g_col, wq2, wkvg2, wo2, g_opm, wlr, wfin, g_in, wproj, wgate, g_mid, wout,
    msa_out, pair_out,
    bsa, bsb, ba, bb, wa, wb32, xn, msah, q, kt, vbd, prob, gate, a32, asend, arecv, xc, pm, pmt, cnt,
    lsend, rsend, lg, rg, r32, rp, lhs2, bd, osend, og, wt, gmt, pad,
    t32, tsend, trecv, tgate, p32, psend, precv, pnow,
    ssem, rsem,
):
    me = lax.axis_index("dap")
    core = lax.rem(me, 2)
    partner = me + 1 - 2 * core
    chip = me // 2
    my_u, my_v = me // LINE, lax.rem(me, LINE)

    x_at, y_at, z_at = me // 32, lax.rem(me // 8, 4), lax.rem(chip, 4)

    def chips():
        for a, b, c in FAR_FIRST:
            yield (
                lax.rem(x_at + a, 4) * 16 + lax.rem(y_at + b, 4) * 4 + lax.rem(z_at + c, 4),
                (a, b, c) == (0, 0, 0),
            )

    def peers():
        for there, here in chips():
            if not here:
                yield there * 2 + core
            yield there * 2 + 1 - core

    barrier = pltpu.get_barrier_semaphore()
    for to in peers():
        pl.semaphore_signal(barrier, inc=1, device_id=(to,), device_id_type=MESH)

    wbt = wb[...]
    pad[...] = jnp.zeros_like(pad)
    for r in range(2):
        pn = norm(pair[r], g_bias[...][None, :]).astype(BF16)
        bt = dot_nt(wbt, pn)
        for j in range(2):
            cols = slice(j * 128, (j + 1) * 128)
            at = (r * 2 + j) * 4
            pad[at : at + 4, :] = bt[0:4, cols]
            pad[BA + at : BA + at + 4, :] = bt[4:8, cols]
    presence = pres[...].astype(F32)
    for r in range(2):
        for j in range(2):
            at = 16 + r * 2 + j
            pad[at : at + 1, :] = presence[r : r + 1, j * 128 : (j + 1) * 128]
    bsa[...] = pad[0:BA, :].astype(BF16)
    bsb[...] = pad[BA : BA + BB, :].astype(BF16)
    ba[core, chip] = bsa[...]
    bb[core, chip] = bsb[...]

    for s in range(2):
        x = norm(msa[s], g_row[...][None, :])
        for c in range(2):
            xn[c] = x[:, c * 128 : (c + 1) * 128]
            msah[s, c] = msa[s, :, c * 128 : (c + 1) * 128]
        xb = x.astype(BF16)
        kt[s] = dot(xb, wkvg1[:, 0:H]).T.astype(BF16)
        spread_heads(dot(xb, wkvg1[:, H : 2 * H]).astype(BF16), vbd, s)
        for r in range(2):
            rows = slice(r * 128, (r + 1) * 128)
            xr = every_other(xn, r).astype(BF16)
            q[s, rows] = (dot(xr, wq1[...]) * SCALE).astype(BF16)
            gate[s, rows] = jax.nn.sigmoid(dot(xr, wkvg1[:, 2 * H :]))

    for w in range(2):
        for c in range(4):
            cols = slice(c * 128, (c + 1) * 128)
            wt[w, cols, :] = wproj[w, :, cols].astype(F32).T.astype(BF16)
        gmt[w] = jnp.broadcast_to(g_mid[w : w + 1, :], (CZ, CZ)).T
    p32[...] = wfin[0:512, :].astype(F32)
    t32[0:512, :] = wfin[512:1024, :].astype(F32)
    bd[...] = jnp.zeros_like(bd)
    for b in range(32):
        part = jnp.concatenate(
            [p32[pl.ds(b, 16, stride=32), :], t32[pl.ds(b, 16, stride=32), :]], axis=0
        ).astype(BF16)
        for i in range(4):
            bd[b * 128 + i * 32 : b * 128 + (i + 1) * 32, i * 128 : (i + 1) * 128] = part

    pl.semaphore_wait(barrier, N - 1)
    for src, dst, sem in ((bsa, ba, 0), (bsb, bb, 10)):
        for there, here in chips():
            if not here:
                send(src, dst.at[core, chip], ssem.at[sem], rsem.at[sem], there * 2 + core)

    pens = [PENALTY * (presence[s : s + 1, :] - 1.0) for s in range(2)]
    for half, (dst, wide, rows_of, sem) in enumerate(((ba, wa, BA, 0), (bb, wb32, BB, 10))):
        landed(dst.at[0, pl.ds(0, N // 2 - 1)], rsem.at[sem])
        send(dst.at[core], dst.at[core], ssem.at[sem + 1], rsem.at[sem + 1], partner)
        landed(dst.at[0], rsem.at[sem + 1])
        landed(dst.at[0, pl.ds(0, N // 2 - 1)], ssem.at[sem])
        landed(dst.at[0], ssem.at[sem + 1])
        for d in range(N):
            wide[d * rows_of : (d + 1) * rows_of, :] = dst[d % 2, d // 2].astype(F32)
        for h in range(4):
            bias = jnp.concatenate(
                [
                    jnp.concatenate(
                        [
                            wide[pl.ds((r * 2 + j) * 4 + h, 128, stride=rows_of), :]
                            for j in range(2)
                        ],
                        axis=1,
                    )
                    for r in range(2)
                ],
                axis=0,
            )
            attend_head(half * 4 + h, q, kt, prob, bias, pens)
    for s in range(2):
        y = (dot(prob[s], vbd[s]) * gate[s]).astype(BF16)
        step = dot(y, wo1[...])
        for r in range(2):
            one = every_other(msah.at[s], r) + step[r * 128 : (r + 1) * 128]
            for c in range(2):
                a32[pl.ds((s * 2 + r) * 2 + c, 128, stride=8), :] = one[:, c * 128 : (c + 1) * 128]
    asend[...] = a32[...].reshape(N, 8, 128).astype(BF16)
    arecv[me] = asend[me]

    def exchange(src, dst, sem):
        for to in peers():
            send(src.at[to], dst.at[me], ssem.at[sem], rsem.at[sem], to)

    def received(src, dst, sem):
        landed(dst.at[pl.ds(0, N - 1)], rsem.at[sem])
        landed(src.at[pl.ds(0, N - 1)], ssem.at[sem])

    exchange(asend, arecv, 2)

    for s in range(2):
        for j in range(2):
            pm[s * 128 : (s + 1) * 128, j * 128 : (j + 1) * 128] = wa[
                pl.ds(16 + s * 2 + j, 128, stride=BA), :
            ]
    pmt[...] = pm[...].T.astype(BF16)
    own = lax.broadcasted_iota(jnp.int32, (16, S), 0) + 2 * me
    hot = (lax.broadcasted_iota(jnp.int32, (16, S), 1) == own).astype(F32).astype(BF16)
    mine = dot(hot, pmt[...])
    pmb = pm[...].astype(BF16)
    for r in range(2):
        hot_c = (lax.broadcasted_iota(jnp.int32, (S, 128), 0) == 2 * me + r).astype(F32)
        col = dot(pmb, hot_c.astype(BF16)).astype(BF16)
        cnt[r] = 1.0 / jnp.maximum(dot(pmt[...], col), 1.0)

    received(asend, arecv, 2)
    a32[...] = arecv[...].astype(F32).reshape(N * 8, 128)
    for r in range(2):
        for s in range(2):
            for c in range(2):
                xc[r, s * 128 : (s + 1) * 128, c * 128 : (c + 1) * 128] = a32[
                    pl.ds((s * 2 + r) * 2 + c, 128, stride=8), :
                ]
        xb = norm(xc[r], g_col[...][None, :]).astype(BF16)
        q[r] = (dot(xb, wq2[...]) * SCALE).astype(BF16)
        kt[r] = dot(xb, wkvg2[:, 0:H]).T.astype(BF16)
        spread_heads(dot(xb, wkvg2[:, H : 2 * H]).astype(BF16), vbd, r)
        gate[r] = jax.nn.sigmoid(dot(xb, wkvg2[:, 2 * H :]))
    pens = [PENALTY * (mine[r : r + 1, :] - 1.0) for r in range(2)]
    for h in range(HEADS):
        attend_head(h, q, kt, prob, None, pens)
    for r in range(2):
        y = (dot(prob[r], vbd[r]) * gate[r]).astype(BF16)
        done = xc[r] + dot(y, wo2[...])
        for s in range(2):
            for c in range(2):
                msa_out[pl.ds(s * 4 + c * 2 + r, 128, stride=8), :] = done[
                    s * 128 : (s + 1) * 128, c * 128 : (c + 1) * 128
                ]
        xb = norm(done, g_opm[...][None, :]).astype(BF16)
        halves = dot_nt(wlr[...], xb) * mine[r : r + 1, :]
        lsend[r * 32 : (r + 1) * 32, :] = halves[0:32].astype(BF16)
        rsend[r * 32 : (r + 1) * 32, :] = halves[32:64].astype(BF16)

    lg[my_u] = lsend[...]
    rg[my_v] = rsend[...]

    def spread_left(i, _):
        send(lsend, lg.at[my_u], ssem.at[3], rsem.at[3], lax.rem(me + LINE * i, N))
        return 0

    def spread_right(i, _):
        to = my_u * LINE + lax.rem(my_v + i, LINE)
        send(rsend, rg.at[my_v], ssem.at[4], rsem.at[4], to)
        return 0

    lax.fori_loop(1, PLANE, spread_left, 0)
    lax.fori_loop(1, LINE, spread_right, 0)
    landed(rg.at[pl.ds(0, LINE - 1)], rsem.at[4])
    for c in range(2):
        r32[c] = rg[:, :, c * 128 : (c + 1) * 128].astype(F32).reshape(512, 128)
    for b in range(32):
        rp[b * 16 : (b + 1) * 16, :] = jnp.concatenate(
            [r32[c, pl.ds(b, 16, stride=32), :] for c in range(2)], axis=1
        ).astype(BF16)
    landed(lg.at[pl.ds(0, PLANE - 1)], rsem.at[3])
    landed(lg.at[pl.ds(0, PLANE - 1)], ssem.at[3])
    landed(rg.at[pl.ds(0, LINE - 1)], ssem.at[4])
    for g in range(8):
        lb = lg[2 * g : 2 * g + 2].reshape(128, S)
        u = dot_nt(rp[...], lb).astype(BF16)
        for b in range(32):
            lhs2[g * 16 : (g + 1) * 16, b * 128 : (b + 1) * 128] = u[b * 16 : (b + 1) * 16]
    block = dot(lhs2[...], bd[...])
    for u in range(PLANE):
        for r in range(2):
            at = 2 * (u % 2) + r
            osend[u, r] = block[
                (u // 2) * 16 : (u // 2 + 1) * 16, at * 128 : (at + 1) * 128
            ].astype(BF16)
    og[my_u] = osend[my_u]

    def give_back(i, _):
        to_u = lax.rem(my_u + i, PLANE)
        send(osend.at[to_u], og.at[my_u], ssem.at[5], rsem.at[5], to_u * LINE + my_v)
        return 0

    lax.fori_loop(1, PLANE, give_back, 0)
    landed(og.at[pl.ds(0, PLANE - 1)], rsem.at[5])
    landed(og.at[pl.ds(0, PLANE - 1)], ssem.at[5])
    for r in range(2):
        delta = og[:, r].astype(F32).reshape(S, CZ)
        pnow[r] = pair[r] + delta * cnt[r]

    lanes = lax.broadcasted_iota(jnp.int32, (1, S), 1)
    am = amino[...].astype(F32)[None, :]
    for w in range(2):
        for r in range(2):
            x = norm(pnow[r], g_in[w : w + 1, :]).astype(BF16)
            here = jnp.sum(jnp.where(lanes == 2 * me + r, am, 0.0), axis=-1, keepdims=True)
            mask = am * here
            pt = dot_nt(wt[w], x)
            for side in range(2):
                at = side * 256
                val = jax.nn.sigmoid(pt[at + 128 : at + 256]) * pt[at : at + 128] * mask
                for j in range(2):
                    t32[pl.ds(side * 4 + r * 2 + j, 128, stride=8), :] = val[
                        :, j * 128 : (j + 1) * 128
                    ]
            tgate[r] = jax.nn.sigmoid(dot(x, wgate[w]))
        tsend[w] = t32[...].reshape(N, 8, 128).astype(BF16)
        trecv[w, me] = tsend[w, me]
        exchange(tsend.at[w], trecv.at[w], 6 + 2 * w)
        received(tsend.at[w], trecv.at[w], 6 + 2 * w)
        t32[...] = trecv[w].astype(F32).reshape(N * 8, 128)
        sides = []
        for side in range(2):
            sides.append(
                jnp.concatenate(
                    [
                        jnp.concatenate(
                            [
                                t32[pl.ds(side * 4 + r * 2 + j, 128, stride=8), :]
                                for j in range(2)
                            ],
                            axis=1,
                        )
                        for r in range(2)
                    ],
                    axis=0,
                )
            )
        if w == 0:
            prod = dot_nt(sides[0].astype(BF16), sides[1].astype(BF16))
        else:
            prod = dot(sides[0].T.astype(BF16), sides[1].astype(BF16))
        for j in range(2):
            xn[j] = prod[:, j * 128 : (j + 1) * 128]
        for r in range(2):
            for j in range(2):
                rows = pl.ds(r * 128, 128) if w == 0 else pl.ds(r, 128, stride=2)
                p32[pl.ds(r * 2 + j, 128, stride=4), :] = xn[j, rows, :]
        psend[w] = p32[...].reshape(N, 4, 128).astype(BF16)
        precv[w, me] = psend[w, me]
        exchange(psend.at[w], precv.at[w], 7 + 2 * w)
        received(psend.at[w], precv.at[w], 7 + 2 * w)
        p32[...] = precv[w].astype(F32).reshape(N * 4, 128)
        for r in range(2):
            for j in range(2):
                pn = norm(p32[pl.ds(r * 2 + j, 128, stride=4), :], gmt[w], axis=0)
                update = dot(pn.T.astype(BF16), wout[w])
                rows = pl.ds(j, 128, stride=2) if w == 0 else pl.ds(j * 128, 128)
                new = pnow[r, rows, :] + update * tgate[r, rows, :]
                if w == 0:
                    pnow[r, rows, :] = new
                else:
                    pair_out[r, rows, :] = new


SCRATCH = [
    ((BA, 128), BF16),
    ((BB, 128), BF16),
    ((2, N // 2, BA, 128), BF16),
    ((2, N // 2, BB, 128), BF16),
    ((N * BA, 128), F32),
    ((N * BB, 128), F32),
    ((2, S, 128), F32),
    ((2, 2, S, 128), F32),
    ((2, S, H), BF16),
    ((2, H, S), BF16),
    ((2, HEADS * S, H), BF16),
    ((2, S, HEADS * S), BF16),
    ((2, S, H), F32),
    ((N * 8, 128), F32),
    ((N, 8, 128), BF16),
    ((N, 8, 128), BF16),
    ((2, S, H), F32),
    ((S, S), F32),
    ((S, S), BF16),
    ((2, S, CZ), F32),
    ((64, S), BF16),
    ((64, S), BF16),
    ((PLANE, 64, S), BF16),
    ((LINE, 64, S), BF16),
    ((2, 512, 128), F32),
    ((512, S), BF16),
    ((128, 4096), BF16),
    ((4096, 512), BF16),
    ((PLANE, 2, 16, 128), BF16),
    ((PLANE, 2, 16, 128), BF16),
    ((2, 512, 128), BF16),
    ((2, CZ, CZ), F32),
    ((BA + BB, 128), F32),
    ((N * 8, 128), F32),
    ((2, N, 8, 128), BF16),
    ((2, N, 8, 128), BF16),
    ((2, S, CZ), F32),
    ((N * 4, 128), F32),
    ((2, N, 4, 128), BF16),
    ((2, N, 4, 128), BF16),
    ((2, S, CZ), F32),
]


def shards(*args):
    vmem = pl.BlockSpec(memory_space=pltpu.VMEM)
    flat, pair = pl.pallas_call(
        body,
        out_shape=(
            jax.ShapeDtypeStruct((S * 4, 128), F32),
            jax.ShapeDtypeStruct((2, S, CZ), F32),
        ),
        in_specs=[vmem] * len(args),
        out_specs=(vmem, vmem),
        scratch_shapes=[pltpu.VMEM(shape, dtype) for shape, dtype in SCRATCH]
        + [pltpu.SemaphoreType.DMA((12,)), pltpu.SemaphoreType.DMA((12,))],
        compiler_params=pltpu.CompilerParams(
            collective_id=0, has_side_effects=True, vmem_limit_bytes=60 << 20
        ),
    )(*args[:9], args[9].T, *args[10:15], args[15].T, *args[16:])
    return flat.reshape(S, 2, 2, 128).transpose(0, 2, 1, 3).reshape(S, 2, H), pair


def solution(mesh):
    rows = P("dap", None, None)
    return jax.shard_map(
        shards,
        mesh=mesh,
        in_specs=(rows, rows, P("dap", None)) + (P(),) * 19,
        out_specs=(P(None, "dap", None), rows),
        check_vma=False,
    )
```

```python
import math

import jax
import jax.numpy as jnp
from jax import lax
from jax.experimental import pallas as pl
from jax.experimental.pallas import tpu as pltpu
from jax.sharding import PartitionSpec as P

N = 128
S = 256
H = 256
CZ = 128
HEADS = 8
WIDTH = 32
PLANE = 16
LINE = 8
BA, BB = 16, 24
N_IN = 22
HOPS = (0, 1, 2, 1)
FAR_FIRST = sorted(
    [(a, b, c) for a in range(4) for b in range(4) for c in range(4)],
    key=lambda o: -(HOPS[o[0]] + HOPS[o[1]] + HOPS[o[2]]),
)
PLANE_FAR_FIRST = sorted(range(1, 16), key=lambda n: -(HOPS[n // 4] + HOPS[n % 4]))
EPS = 1e-05
PENALTY = 1e9
SCALE = 1.0 / math.sqrt(WIDTH)
F32, BF16 = jnp.float32, jnp.bfloat16
MESH = pl.DeviceIdType.MESH


def dot(a, b):
    return jnp.dot(a, b, preferred_element_type=F32)


def dot_nt(a, b):
    return lax.dot_general(a, b, (((1,), (1,)), ((), ())), preferred_element_type=F32)


def norm(x, gain, axis=-1):
    centred = x - jnp.mean(x, axis=axis, keepdims=True)
    spread = jnp.mean(centred * centred, axis=axis, keepdims=True)
    return centred * lax.rsqrt(spread + EPS) * gain


def send(src, dst, ssem, rsem, to):
    pltpu.make_async_remote_copy(
        src_ref=src, dst_ref=dst, send_sem=ssem, recv_sem=rsem, device_id=(to,), device_id_type=MESH
    ).start()


def landed(like, sem):
    pltpu.make_async_copy(like, like, sem).wait()


def every_other(halves, first):
    return jnp.concatenate([halves[c, pl.ds(first, 128, stride=2), :] for c in range(2)], axis=1)


def head_lanes(h):
    lanes = lax.broadcasted_iota(jnp.int32, (1, H), 1)
    return jnp.logical_and(lanes >= h * WIDTH, lanes < (h + 1) * WIDTH).astype(F32).astype(BF16)


def spread_heads(v, vbd, t):
    for h in range(HEADS):
        vbd[t, h * S : (h + 1) * S, :] = v * head_lanes(h)


def attend_head(h, t, q, kt, prob, bias, pen):
    scores = dot(q[t] * head_lanes(h), kt[t])
    if bias is not None:
        scores = scores + bias
    scores = scores + pen
    top = jnp.max(scores, axis=-1, keepdims=True)
    e = jnp.exp(scores - top)
    prob[t, :, h * S : (h + 1) * S] = (e * (1.0 / jnp.sum(e, axis=-1, keepdims=True))).astype(BF16)


def body(*refs):
    ins, outs, refs = refs[:N_IN], refs[N_IN : N_IN + 2], refs[N_IN + 2 :]
    here, refs = refs[:N_IN], refs[N_IN:]
    (
        msa, pair, pres, amino, g_row, wq1, wkvg1, wo1, g_bias, wb, g_col,
        wq2, wkvg2, wo2, g_opm, wlr, wfin, g_in, wproj, wgate, g_mid, wout,
    ) = here
    (
        msa_out, pair_out, bsa, bsb, ba, bb, wa, wb32, xn, msah, q, kt, vbd, prob, gate, a32,
        asend, arecv, xc, pm, pmt, cnt, lsend, rsend, lg, rg, r32, rp, lhs2, bd, osend, og,
        wt, gmt, pad, t32, tsend, trecv, tgate, p32, psend, precv, pnow,
        ssem, rsem, isem, osem,
    ) = refs
    me = lax.axis_index("dap")
    core = lax.rem(me, 2)
    partner = me + 1 - 2 * core
    chip = me // 2
    my_u, my_v = me // LINE, lax.rem(me, LINE)

    x_at, y_at, z_at = me // 32, lax.rem(me // 8, 4), lax.rem(chip, 4)

    def chips():
        for a, b, c in FAR_FIRST:
            yield (
                lax.rem(x_at + a, 4) * 16 + lax.rem(y_at + b, 4) * 4 + lax.rem(z_at + c, 4),
                (a, b, c) == (0, 0, 0),
            )

    def peers():
        for there, here in chips():
            if not here:
                yield there * 2 + core
            yield there * 2 + 1 - core

    barrier = pltpu.get_barrier_semaphore()
    for to in peers():
        pl.semaphore_signal(barrier, inc=1, device_id=(to,), device_id_type=MESH)

    order = (1, 8, 9, 2, 0, 4, 5, 6, 18, 20, 16, 7, 3, 10, 11, 12, 13, 14, 15, 17, 19, 21)
    for n in order:
        pltpu.make_async_copy(ins[n], here[n], isem.at[n]).start()

    def arrived(*which):
        for n in which:
            pltpu.make_async_copy(ins[n], here[n], isem.at[n]).wait()

    arrived(1, 8, 9, 2)
    wbt = wb[...]
    pad[...] = jnp.zeros_like(pad)
    for r in range(2):
        pn = norm(pair[r], g_bias[...]).astype(BF16)
        bt = dot_nt(wbt, pn)
        for j in range(2):
            cols = slice(j * 128, (j + 1) * 128)
            at = (r * 2 + j) * 4
            pad[at : at + 4, :] = bt[0:4, cols]
            pad[BA + at : BA + at + 4, :] = bt[4:8, cols]
    presence = pres[...].astype(F32)
    for r in range(2):
        for j in range(2):
            at = BA + 16 + r * 2 + j
            pad[at : at + 1, :] = presence[r : r + 1, j * 128 : (j + 1) * 128]
    bsa[...] = pad[0:BA, :].astype(BF16)
    bsb[...] = pad[BA : BA + BB, :].astype(BF16)
    ba[core, chip] = bsa[...]
    bb[core, chip] = bsb[...]

    arrived(0, 4, 5, 6)
    for s in range(2):
        x = norm(msa[s], g_row[...])
        for c in range(2):
            xn[c] = x[:, c * 128 : (c + 1) * 128]
            msah[s, c] = msa[s, :, c * 128 : (c + 1) * 128]
        xb = x.astype(BF16)
        kt[s] = dot(xb, wkvg1[:, 0:H]).T.astype(BF16)
        spread_heads(dot(xb, wkvg1[:, H : 2 * H]).astype(BF16), vbd, s)
        for r in range(2):
            rows = slice(r * 128, (r + 1) * 128)
            xr = every_other(xn, r).astype(BF16)
            q[s, rows] = (dot(xr, wq1[...]) * SCALE).astype(BF16)
            gate[s, rows] = jax.nn.sigmoid(dot(xr, wkvg1[:, 2 * H :]))

    arrived(18, 20, 16, 7, 3, 10, 11, 12, 13, 14, 15, 17, 19, 21)
    for w in range(2):
        for c in range(4):
            cols = slice(c * 128, (c + 1) * 128)
            wt[w, cols, :] = wproj[w, :, cols].astype(F32).T.astype(BF16)
        gmt[w] = jnp.broadcast_to(g_mid[w : w + 1, :], (CZ, CZ)).T
    p32[...] = wfin[0:512, :].astype(F32)
    t32[0:512, :] = wfin[512:1024, :].astype(F32)
    bd[...] = jnp.zeros_like(bd)
    for b in range(32):
        part = jnp.concatenate(
            [p32[pl.ds(b, 16, stride=32), :], t32[pl.ds(b, 16, stride=32), :]], axis=0
        ).astype(BF16)
        for i in range(4):
            bd[b * 128 + i * 32 : b * 128 + (i + 1) * 32, i * 128 : (i + 1) * 128] = part

    pl.semaphore_wait(barrier, N - 1)
    for src, dst, sem in ((bsa, ba, 0), (bsb, bb, 10)):
        for there, here in chips():
            if not here:
                send(src, dst.at[core, chip], ssem.at[sem], rsem.at[sem], there * 2 + core)

    pens = [PENALTY * (presence[s : s + 1, :] - 1.0) for s in range(2)]
    halves = ((ba, wa, BA, 0), (bb, wb32, BB, 10))

    def swap(dst, sem):
        landed(dst.at[0, pl.ds(0, N // 2 - 1)], rsem.at[sem])
        send(dst.at[core], dst.at[core], ssem.at[sem + 1], rsem.at[sem + 1], partner)

    swap(ba, 0)
    for half, (dst, wide, rows_of, sem) in enumerate(halves):
        landed(dst.at[0], rsem.at[sem + 1])
        landed(dst.at[0, pl.ds(0, N // 2 - 1)], ssem.at[sem])
        landed(dst.at[0], ssem.at[sem + 1])
        for d in range(N):
            wide[d * rows_of : (d + 1) * rows_of, :] = dst[d % 2, d // 2].astype(F32)
        for h in range(4):
            bias = jnp.concatenate(
                [
                    jnp.concatenate(
                        [
                            wide[pl.ds((r * 2 + j) * 4 + h, 128, stride=rows_of), :]
                            for j in range(2)
                        ],
                        axis=1,
                    )
                    for r in range(2)
                ],
                axis=0,
            )
            for t in range(2):
                attend_head(half * 4 + h, t, q, kt, prob, bias, pens[t])
            if half == 0 and h == 1:
                swap(bb, 10)
    for s in range(2):
        y = (dot(prob[s], vbd[s]) * gate[s]).astype(BF16)
        step = dot(y, wo1[...])
        for r in range(2):
            one = every_other(msah.at[s], r) + step[r * 128 : (r + 1) * 128]
            for c in range(2):
                a32[pl.ds((s * 2 + r) * 2 + c, 128, stride=8), :] = one[:, c * 128 : (c + 1) * 128]
    asend[...] = a32[...].reshape(N, 8, 128).astype(BF16)
    arecv[me] = asend[me]

    def exchange(src, dst, sem):
        for to in peers():
            send(src.at[to], dst.at[me], ssem.at[sem], rsem.at[sem], to)

    def received(src, dst, sem):
        landed(dst.at[pl.ds(0, N - 1)], rsem.at[sem])
        landed(src.at[pl.ds(0, N - 1)], ssem.at[sem])

    exchange(asend, arecv, 2)

    for s in range(2):
        for j in range(2):
            pm[s * 128 : (s + 1) * 128, j * 128 : (j + 1) * 128] = wb32[
                pl.ds(16 + s * 2 + j, 128, stride=BB), :
            ]
    pmt[...] = pm[...].T.astype(BF16)
    own = lax.broadcasted_iota(jnp.int32, (16, S), 0) + 2 * me
    hot = (lax.broadcasted_iota(jnp.int32, (16, S), 1) == own).astype(F32).astype(BF16)
    mine = dot(hot, pmt[...])
    pmb = pm[...].astype(BF16)
    for r in range(2):
        hot_c = (lax.broadcasted_iota(jnp.int32, (S, 128), 0) == 2 * me + r).astype(F32)
        col = dot(pmb, hot_c.astype(BF16)).astype(BF16)
        cnt[r] = 1.0 / jnp.maximum(dot(pmt[...], col), 1.0)

    received(asend, arecv, 2)
    a32[...] = arecv[...].astype(F32).reshape(N * 8, 128)
    for r in range(2):
        for s in range(2):
            for c in range(2):
                xc[r, s * 128 : (s + 1) * 128, c * 128 : (c + 1) * 128] = a32[
                    pl.ds((s * 2 + r) * 2 + c, 128, stride=8), :
                ]
        xb = norm(xc[r], g_col[...]).astype(BF16)
        q[r] = (dot(xb, wq2[...]) * SCALE).astype(BF16)
        kt[r] = dot(xb, wkvg2[:, 0:H]).T.astype(BF16)
        spread_heads(dot(xb, wkvg2[:, H : 2 * H]).astype(BF16), vbd, r)
        gate[r] = jax.nn.sigmoid(dot(xb, wkvg2[:, 2 * H :]))
    for r in range(2):
        for h in range(HEADS):
            attend_head(h, r, q, kt, prob, None, PENALTY * (mine[r : r + 1, :] - 1.0))
        y = (dot(prob[r], vbd[r]) * gate[r]).astype(BF16)
        done = xc[r] + dot(y, wo2[...])
        for s in range(2):
            for c in range(2):
                msa_out[pl.ds(s * 4 + c * 2 + r, 128, stride=8), :] = done[
                    s * 128 : (s + 1) * 128, c * 128 : (c + 1) * 128
                ]
        xb = norm(done, g_opm[...]).astype(BF16)
        projected = dot_nt(wlr[...], xb) * mine[r : r + 1, :]
        lsend[r] = projected[0:32].astype(BF16)
        rsend[r] = projected[32:64].astype(BF16)
        lg[r, my_u] = lsend[r]
        if r == 1:
            rg[my_v] = rsend[...]
            for n in range(1, LINE):
                send(
                    rsend, rg.at[my_v], ssem.at[4], rsem.at[4],
                    my_u * LINE + lax.rem(my_v + n, LINE),
                )
        for n in PLANE_FAR_FIRST:
            to = lax.rem(x_at + n // 4, 4) * 32 + lax.rem(y_at + n % 4, 4) * 8 + my_v
            send(lsend.at[r], lg.at[r, my_u], ssem.at[3 + 9 * r], rsem.at[3 + 9 * r], to)
    pltpu.make_async_copy(msa_out, outs[0], osem.at[0]).start()

    landed(rg.at[pl.ds(0, LINE - 1)], rsem.at[4])
    for c in range(2):
        r32[c] = rg[:, :, :, c * 128 : (c + 1) * 128].astype(F32).reshape(512, 128)
    for b in range(32):
        rp[b * 16 : (b + 1) * 16, :] = jnp.concatenate(
            [r32[c, pl.ds(b, 16, stride=32), :] for c in range(2)], axis=1
        ).astype(BF16)
    for r in range(2):
        for sems in (rsem, ssem):
            landed(lg.at[0, pl.ds(0, PLANE - 1)], sems.at[3 + 9 * r])
        for g in range(4):
            lb = lg[r, 4 * g : 4 * g + 4].reshape(128, S)
            u = dot_nt(rp[...], lb).astype(BF16)
            at = (r * 4 + g) * 16
            for b in range(32):
                lhs2[at : at + 16, b * 128 : (b + 1) * 128] = u[b * 16 : (b + 1) * 16]
    landed(rg.at[pl.ds(0, LINE - 1)], ssem.at[4])
    block = dot(lhs2[...], bd[...])
    for u in range(PLANE):
        for r in range(2):
            row, at = (r * 4 + u // 4) * 16, u % 4
            osend[u, r] = block[row : row + 16, at * 128 : (at + 1) * 128].astype(BF16)
    og[my_u] = osend[my_u]

    for n in PLANE_FAR_FIRST:
        to_u = lax.rem(x_at + n // 4, 4) * 4 + lax.rem(y_at + n % 4, 4)
        send(osend.at[to_u], og.at[my_u], ssem.at[5], rsem.at[5], to_u * LINE + my_v)
    landed(og.at[pl.ds(0, PLANE - 1)], rsem.at[5])
    landed(og.at[pl.ds(0, PLANE - 1)], ssem.at[5])
    for r in range(2):
        delta = og[:, r].astype(F32).reshape(S, CZ)
        pnow[r] = pair[r] + delta * cnt[r]

    lanes = lax.broadcasted_iota(jnp.int32, (1, S), 1)
    am = amino[...].astype(F32)
    for w in range(2):
        for r in range(2):
            x = norm(pnow[r], g_in[w : w + 1, :]).astype(BF16)
            here = jnp.sum(jnp.where(lanes == 2 * me + r, am, 0.0), axis=-1, keepdims=True)
            mask = am * here
            pt = dot_nt(wt[w], x)
            for side in range(2):
                at = side * 256
                val = jax.nn.sigmoid(pt[at + 128 : at + 256]) * pt[at : at + 128] * mask
                for j in range(2):
                    t32[pl.ds(side * 4 + r * 2 + j, 128, stride=8), :] = val[
                        :, j * 128 : (j + 1) * 128
                    ]
            tgate[r] = jax.nn.sigmoid(dot(x, wgate[w]))
        tsend[w] = t32[...].reshape(N, 8, 128).astype(BF16)
        trecv[w, me] = tsend[w, me]
        exchange(tsend.at[w], trecv.at[w], 6 + 2 * w)
        received(tsend.at[w], trecv.at[w], 6 + 2 * w)
        t32[...] = trecv[w].astype(F32).reshape(N * 8, 128)
        sides = []
        for side in range(2):
            sides.append(
                jnp.concatenate(
                    [
                        jnp.concatenate(
                            [
                                t32[pl.ds(side * 4 + r * 2 + j, 128, stride=8), :]
                                for j in range(2)
                            ],
                            axis=1,
                        )
                        for r in range(2)
                    ],
                    axis=0,
                )
            )
        if w == 0:
            prod = dot_nt(sides[0].astype(BF16), sides[1].astype(BF16))
        else:
            prod = dot(sides[0].T.astype(BF16), sides[1].astype(BF16))
        for j in range(2):
            xn[j] = prod[:, j * 128 : (j + 1) * 128]
        for r in range(2):
            for j in range(2):
                rows = pl.ds(r * 128, 128) if w == 0 else pl.ds(r, 128, stride=2)
                p32[pl.ds(r * 2 + j, 128, stride=4), :] = xn[j, rows, :]
        psend[w] = p32[...].reshape(N, 4, 128).astype(BF16)
        precv[w, me] = psend[w, me]
        exchange(psend.at[w], precv.at[w], 7 + 2 * w)
        received(psend.at[w], precv.at[w], 7 + 2 * w)
        p32[...] = precv[w].astype(F32).reshape(N * 4, 128)
        for r in range(2):
            for j in range(2):
                pn = norm(p32[pl.ds(r * 2 + j, 128, stride=4), :], gmt[w], axis=0)
                update = dot(pn.T.astype(BF16), wout[w])
                rows = pl.ds(j, 128, stride=2) if w == 0 else pl.ds(j * 128, 128)
                new = pnow[r, rows, :] + update * tgate[r, rows, :]
                if w == 0:
                    pnow[r, rows, :] = new
                else:
                    pair_out[r, rows, :] = new
            if w == 1:
                pltpu.make_async_copy(pair_out.at[r], outs[1].at[r], osem.at[1 + r]).start()
    pltpu.make_async_copy(msa_out, outs[0], osem.at[0]).wait()
    for r in range(2):
        pltpu.make_async_copy(pair_out.at[r], outs[1].at[r], osem.at[1 + r]).wait()


def copied(a, b, a_out, b_out, a_here, b_here, sems):
    moves = []
    for n in range(4):
        part = pl.ds(n * 256, 256)
        moves.append((a.at[part], a_here.at[part], a_out.at[part]))
    for n in range(2):
        moves.append((b.at[n], b_here.at[n], b_out.at[n]))
    for n, (src, here, _) in enumerate(moves):
        pltpu.make_async_copy(src, here, sems.at[n]).start()
    for n, (src, here, dst) in enumerate(moves):
        pltpu.make_async_copy(src, here, sems.at[n]).wait()
        pltpu.make_async_copy(here, dst, sems.at[6 + n]).start()
    for n, (_, here, dst) in enumerate(moves):
        pltpu.make_async_copy(here, dst, sems.at[6 + n]).wait()


SCRATCH = [
    ((S * 4, 128), F32),
    ((2, S, CZ), F32),
    ((BA, 128), BF16),
    ((BB, 128), BF16),
    ((2, N // 2, BA, 128), BF16),
    ((2, N // 2, BB, 128), BF16),
    ((N * BA, 128), F32),
    ((N * BB, 128), F32),
    ((2, S, 128), F32),
    ((2, 2, S, 128), F32),
    ((2, S, H), BF16),
    ((2, H, S), BF16),
    ((2, HEADS * S, H), BF16),
    ((2, S, HEADS * S), BF16),
    ((2, S, H), F32),
    ((N * 8, 128), F32),
    ((N, 8, 128), BF16),
    ((N, 8, 128), BF16),
    ((2, S, H), F32),
    ((S, S), F32),
    ((S, S), BF16),
    ((2, S, CZ), F32),
    ((2, 32, S), BF16),
    ((2, 32, S), BF16),
    ((2, PLANE, 32, S), BF16),
    ((LINE, 2, 32, S), BF16),
    ((2, 512, 128), F32),
    ((512, S), BF16),
    ((128, 4096), BF16),
    ((4096, 512), BF16),
    ((PLANE, 2, 16, 128), BF16),
    ((PLANE, 2, 16, 128), BF16),
    ((2, 512, 128), BF16),
    ((2, CZ, CZ), F32),
    ((BA + BB, 128), F32),
    ((N * 8, 128), F32),
    ((2, N, 8, 128), BF16),
    ((2, N, 8, 128), BF16),
    ((2, S, CZ), F32),
    ((N * 4, 128), F32),
    ((2, N, 4, 128), BF16),
    ((2, N, 4, 128), BF16),
    ((2, S, CZ), F32),
]


def shards(*args):
    args = [a.reshape(1, -1) if a.ndim == 1 else a for a in args]
    for n in (9, 15):
        args[n] = args[n].T
    anywhere = pl.BlockSpec(memory_space=pl.ANY)
    results = (
        jax.ShapeDtypeStruct((S * 4, 128), F32),
        jax.ShapeDtypeStruct((2, S, CZ), F32),
    )
    flat, pair = pl.pallas_call(
        body,
        out_shape=results,
        in_specs=[anywhere] * N_IN,
        out_specs=(anywhere, anywhere),
        scratch_shapes=[pltpu.VMEM(a.shape, a.dtype) for a in args]
        + [pltpu.VMEM(shape, dtype) for shape, dtype in SCRATCH]
        + [pltpu.SemaphoreType.DMA((n,)) for n in (13, 13, N_IN, 3)],
        compiler_params=pltpu.CompilerParams(
            collective_id=0, has_side_effects=True, vmem_limit_bytes=60 << 20
        ),
    )(*args)
    flat, pair = pl.pallas_call(
        copied,
        out_shape=results,
        in_specs=[anywhere] * 2,
        out_specs=(anywhere, anywhere),
        scratch_shapes=[pltpu.VMEM(a.shape, a.dtype) for a in results]
        + [pltpu.SemaphoreType.DMA((12,))],
    )(flat, pair)
    return flat.reshape(S, 2, 2, 128).transpose(0, 2, 1, 3).reshape(S, 2, H), pair


def solution(mesh):
    rows = P("dap", None, None)
    return jax.shard_map(
        shards,
        mesh=mesh,
        in_specs=(rows, rows, P("dap", None)) + (P(),) * 19,
        out_specs=(P(None, "dap", None), rows),
        check_vma=False,
    )
```

```python
import math

import jax
import jax.numpy as jnp
from jax import lax
from jax.experimental import pallas as pl
from jax.experimental.pallas import tpu as pltpu
from jax.sharding import PartitionSpec as P

N = 128
S = 256
H = 256
CZ = 128
HEADS = 8
WIDTH = 32
PLANE = 16
LINE = 8
BA, BB = 16, 24
N_IN = 22
HOPS = (0, 1, 2, 1)
FAR_FIRST = sorted(
    [(a, b, c) for a in range(4) for b in range(4) for c in range(4)],
    key=lambda o: -(HOPS[o[0]] + HOPS[o[1]] + HOPS[o[2]]),
)
PLANE_FAR_FIRST = sorted(range(1, 16), key=lambda n: -(HOPS[n // 4] + HOPS[n % 4]))
EPS = 1e-05
PENALTY = 1e9
SCALE = 1.0 / math.sqrt(WIDTH)
F32, BF16 = jnp.float32, jnp.bfloat16
MESH = pl.DeviceIdType.MESH


def dot(a, b):
    return jnp.dot(a, b, preferred_element_type=F32)


def dot_nt(a, b):
    return lax.dot_general(a, b, (((1,), (1,)), ((), ())), preferred_element_type=F32)


def norm(x, gain, axis=-1):
    centred = x - jnp.mean(x, axis=axis, keepdims=True)
    spread = jnp.mean(centred * centred, axis=axis, keepdims=True)
    return centred * lax.rsqrt(spread + EPS) * gain


def send(src, dst, ssem, rsem, to):
    pltpu.make_async_remote_copy(
        src_ref=src, dst_ref=dst, send_sem=ssem, recv_sem=rsem, device_id=(to,), device_id_type=MESH
    ).start()


def landed(like, sem):
    pltpu.make_async_copy(like, like, sem).wait()


def every_other(halves, first):
    return jnp.concatenate([halves[c, pl.ds(first, 128, stride=2), :] for c in range(2)], axis=1)


def head_lanes(h):
    lanes = lax.broadcasted_iota(jnp.int32, (1, H), 1)
    return jnp.logical_and(lanes >= h * WIDTH, lanes < (h + 1) * WIDTH).astype(F32).astype(BF16)


def spread_heads(v, vbd, t):
    for h in range(HEADS):
        vbd[t, h * S : (h + 1) * S, :] = v * head_lanes(h)


def attend_head(h, t, q, kt, prob, bias, pen):
    scores = dot(q[t] * head_lanes(h), kt[t])
    if bias is not None:
        scores = scores + bias
    scores = scores + pen
    top = jnp.max(scores, axis=-1, keepdims=True)
    e = jnp.exp(scores - top)
    prob[t, :, h * S : (h + 1) * S] = (e * (1.0 / jnp.sum(e, axis=-1, keepdims=True))).astype(BF16)


def body(*refs):
    ins, outs, refs = refs[:N_IN], refs[N_IN : N_IN + 2], refs[N_IN + 2 :]
    here, refs = refs[:N_IN], refs[N_IN:]
    msa_out, pair_out = outs
    (
        msa, pair, pres, amino, g_row, wq1, wkvg1, wo1, g_bias, wb, g_col,
        wq2, wkvg2, wo2, g_opm, wlr, wfin, g_in, wproj, wgate, g_mid, wout,
    ) = here
    (
        bsa, bsb, ba, bb, wa, wb32, xn, msah, q, kt, vbd, prob, gate, a32,
        asend, arecv, xc, pm, pmt, cnt, lsend, rsend, lg, rg, r32, rp, lhs2, bd, osend, og,
        wt, gmt, pad, t32, tsend, trecv, tgate, p32, psend, precv, pnow,
        ssem, rsem, isem,
    ) = refs
    me = lax.axis_index("dap")
    core = lax.rem(me, 2)
    partner = me + 1 - 2 * core
    chip = me // 2
    my_u, my_v = me // LINE, lax.rem(me, LINE)

    x_at, y_at, z_at = me // 32, lax.rem(me // 8, 4), lax.rem(chip, 4)

    def chips():
        for a, b, c in FAR_FIRST:
            yield (
                lax.rem(x_at + a, 4) * 16 + lax.rem(y_at + b, 4) * 4 + lax.rem(z_at + c, 4),
                (a, b, c) == (0, 0, 0),
            )

    def peers():
        for there, here in chips():
            if not here:
                yield there * 2 + core
            yield there * 2 + 1 - core

    def plane():
        for n in PLANE_FAR_FIRST:
            yield lax.rem(x_at + n // 4, 4) * 4 + lax.rem(y_at + n % 4, 4)

    def line():
        for n in (2, 1, 3, 0):
            if n:
                yield lax.rem(z_at + n, 4) * 2 + core
            yield lax.rem(z_at + n, 4) * 2 + 1 - core

    barrier = pltpu.get_barrier_semaphore()
    for to in peers():
        pl.semaphore_signal(barrier, inc=1, device_id=(to,), device_id_type=MESH)

    order = (1, 8, 9, 2, 0, 4, 5, 6, 18, 20, 16, 7, 3, 10, 11, 12, 13, 14, 15, 17, 19, 21)
    for n in order:
        pltpu.make_async_copy(ins[n], here[n], isem.at[n]).start()

    def arrived(*which):
        for n in which:
            pltpu.make_async_copy(ins[n], here[n], isem.at[n]).wait()

    arrived(1, 8, 9, 2)
    wbt = wb[...]
    pad[...] = jnp.zeros_like(pad)
    for r in range(2):
        pn = norm(pair[r], g_bias[...]).astype(BF16)
        bt = dot_nt(wbt, pn)
        for j in range(2):
            cols = slice(j * 128, (j + 1) * 128)
            at = (r * 2 + j) * 4
            pad[at : at + 4, :] = bt[0:4, cols]
            pad[BA + at : BA + at + 4, :] = bt[4:8, cols]
    presence = pres[...].astype(F32)
    for r in range(2):
        for j in range(2):
            at = BA + 16 + r * 2 + j
            pad[at : at + 1, :] = presence[r : r + 1, j * 128 : (j + 1) * 128]
    bsa[...] = pad[0:BA, :].astype(BF16)
    bsb[...] = pad[BA : BA + BB, :].astype(BF16)
    ba[core, chip] = bsa[...]
    bb[core, chip] = bsb[...]

    arrived(0, 4, 5, 6)
    for s in range(2):
        x = norm(msa[s], g_row[...])
        for c in range(2):
            xn[c] = x[:, c * 128 : (c + 1) * 128]
            msah[s, c] = msa[s, :, c * 128 : (c + 1) * 128]
        xb = x.astype(BF16)
        kt[s] = dot(xb, wkvg1[:, 0:H]).T.astype(BF16)
        spread_heads(dot(xb, wkvg1[:, H : 2 * H]).astype(BF16), vbd, s)
        for r in range(2):
            rows = slice(r * 128, (r + 1) * 128)
            xr = every_other(xn, r).astype(BF16)
            q[s, rows] = (dot(xr, wq1[...]) * SCALE).astype(BF16)
            gate[s, rows] = jax.nn.sigmoid(dot(xr, wkvg1[:, 2 * H :]))

    arrived(18, 20, 16, 7, 3, 10, 11, 12, 13, 14, 15, 17, 19, 21)
    for w in range(2):
        for c in range(4):
            cols = slice(c * 128, (c + 1) * 128)
            wt[w, cols, :] = wproj[w, :, cols].astype(F32).T.astype(BF16)
        gmt[w] = jnp.broadcast_to(g_mid[w : w + 1, :], (CZ, CZ)).T
    p32[...] = wfin[0:512, :].astype(F32)
    t32[0:512, :] = wfin[512:1024, :].astype(F32)
    bd[...] = jnp.zeros_like(bd)
    for b in range(32):
        part = jnp.concatenate(
            [p32[pl.ds(b, 16, stride=32), :], t32[pl.ds(b, 16, stride=32), :]], axis=0
        ).astype(BF16)
        for i in range(4):
            bd[b * 128 + i * 32 : b * 128 + (i + 1) * 32, i * 128 : (i + 1) * 128] = part

    pl.semaphore_wait(barrier, N - 1)
    for src, dst, sem in ((bsa, ba, 0), (bsb, bb, 10)):
        for there, here in chips():
            if not here:
                send(src, dst.at[core, chip], ssem.at[sem], rsem.at[sem], there * 2 + core)

    pens = [PENALTY * (presence[s : s + 1, :] - 1.0) for s in range(2)]
    halves = ((ba, wa, BA, 0), (bb, wb32, BB, 10))

    def swap(dst, sem):
        landed(dst.at[0, pl.ds(0, N // 2 - 1)], rsem.at[sem])
        send(dst.at[core], dst.at[core], ssem.at[sem + 1], rsem.at[sem + 1], partner)

    swap(ba, 0)
    for half, (dst, wide, rows_of, sem) in enumerate(halves):
        landed(dst.at[0], rsem.at[sem + 1])
        landed(dst.at[0, pl.ds(0, N // 2 - 1)], ssem.at[sem])
        landed(dst.at[0], ssem.at[sem + 1])
        for d in range(N):
            wide[d * rows_of : (d + 1) * rows_of, :] = dst[d % 2, d // 2].astype(F32)
        for h in range(4):
            bias = jnp.concatenate(
                [
                    jnp.concatenate(
                        [
                            wide[pl.ds((r * 2 + j) * 4 + h, 128, stride=rows_of), :]
                            for j in range(2)
                        ],
                        axis=1,
                    )
                    for r in range(2)
                ],
                axis=0,
            )
            for t in range(2):
                attend_head(half * 4 + h, t, q, kt, prob, bias, pens[t])
            if half == 0 and h == 1:
                swap(bb, 10)
    for s in range(2):
        y = (dot(prob[s], vbd[s]) * gate[s]).astype(BF16)
        step = dot(y, wo1[...])
        for r in range(2):
            one = every_other(msah.at[s], r) + step[r * 128 : (r + 1) * 128]
            for c in range(2):
                a32[pl.ds((s * 2 + r) * 2 + c, 128, stride=8), :] = one[:, c * 128 : (c + 1) * 128]
    asend[...] = a32[...].reshape(N, 8, 128).astype(BF16)
    arecv[me] = asend[me]

    def exchange(src, dst, sem):
        for to in peers():
            send(src.at[to], dst.at[me], ssem.at[sem], rsem.at[sem], to)

    def received(src, dst, sem):
        landed(dst.at[pl.ds(0, N - 1)], rsem.at[sem])
        landed(src.at[pl.ds(0, N - 1)], ssem.at[sem])

    exchange(asend, arecv, 2)

    for s in range(2):
        for j in range(2):
            pm[s * 128 : (s + 1) * 128, j * 128 : (j + 1) * 128] = wb32[
                pl.ds(16 + s * 2 + j, 128, stride=BB), :
            ]
    pmt[...] = pm[...].T.astype(BF16)
    own = lax.broadcasted_iota(jnp.int32, (16, S), 0) + 2 * me
    hot = (lax.broadcasted_iota(jnp.int32, (16, S), 1) == own).astype(F32).astype(BF16)
    mine = dot(hot, pmt[...])
    pmb = pm[...].astype(BF16)
    for r in range(2):
        hot_c = (lax.broadcasted_iota(jnp.int32, (S, 128), 0) == 2 * me + r).astype(F32)
        col = dot(pmb, hot_c.astype(BF16)).astype(BF16)
        cnt[r] = 1.0 / jnp.maximum(dot(pmt[...], col), 1.0)

    received(asend, arecv, 2)
    a32[...] = arecv[...].astype(F32).reshape(N * 8, 128)
    for r in range(2):
        for s in range(2):
            for c in range(2):
                xc[r, s * 128 : (s + 1) * 128, c * 128 : (c + 1) * 128] = a32[
                    pl.ds((s * 2 + r) * 2 + c, 128, stride=8), :
                ]
        xb = norm(xc[r], g_col[...]).astype(BF16)
        q[r] = (dot(xb, wq2[...]) * SCALE).astype(BF16)
        kt[r] = dot(xb, wkvg2[:, 0:H]).T.astype(BF16)
        spread_heads(dot(xb, wkvg2[:, H : 2 * H]).astype(BF16), vbd, r)
        gate[r] = jax.nn.sigmoid(dot(xb, wkvg2[:, 2 * H :]))
    for r in range(2):
        for h in range(HEADS):
            attend_head(h, r, q, kt, prob, None, PENALTY * (mine[r : r + 1, :] - 1.0))
        y = (dot(prob[r], vbd[r]) * gate[r]).astype(BF16)
        done = xc[r] + dot(y, wo2[...])
        for s in range(2):
            for c in range(2):
                msa_out[pl.ds(s * 4 + c * 2 + r, 128, stride=8), :] = done[
                    s * 128 : (s + 1) * 128, c * 128 : (c + 1) * 128
                ]
        xb = norm(done, g_opm[...]).astype(BF16)
        projected = dot_nt(wlr[...], xb) * mine[r : r + 1, :]
        lsend[r] = projected[0:32].astype(BF16)
        rsend[r] = projected[32:64].astype(BF16)
        rg[r, my_u] = rsend[r]
        if r == 1:
            lg[my_v] = lsend[...]
            for to_v in line():
                send(lsend, lg.at[my_v], ssem.at[4], rsem.at[4], my_u * LINE + to_v)
        for to_u in plane():
            to = to_u * LINE + my_v
            send(rsend.at[r], rg.at[r, my_u], ssem.at[3 + 9 * r], rsem.at[3 + 9 * r], to)

    for r in range(2):
        for sems in (rsem, ssem):
            landed(rg.at[0, pl.ds(0, PLANE - 1)], sems.at[3 + 9 * r])
        for c in range(2):
            r32[c] = rg[r, :, :, c * 128 : (c + 1) * 128].astype(F32).reshape(512, 128)
        for b in range(32):
            rp[r, b * 16 : (b + 1) * 16, :] = jnp.concatenate(
                [r32[c, pl.ds(b, 16, stride=32), :] for c in range(2)], axis=1
            ).astype(BF16)
        if r == 0:
            for sems in (rsem, ssem):
                landed(lg.at[pl.ds(0, LINE - 1)], sems.at[4])
        for g in range(4):
            lb = lg[2 * g : 2 * g + 2].reshape(128, S)
            u = dot_nt(rp[r], lb).astype(BF16)
            at = g * 32 + r * 16
            for b in range(32):
                lhs2[at : at + 16, b * 128 : (b + 1) * 128] = u[b * 16 : (b + 1) * 16]
    block = dot(lhs2[...], bd[...])
    for to_v in range(LINE):
        for r in range(2):
            row, at = (to_v // 2) * 32, (to_v % 2) * 2 + r
            osend[to_v, r] = block[row : row + 32, at * 128 : (at + 1) * 128].astype(BF16)
    og[my_v] = osend[my_v]
    for to_v in line():
        send(osend.at[to_v], og.at[my_v], ssem.at[5], rsem.at[5], my_u * LINE + to_v)
    for sems in (rsem, ssem):
        landed(og.at[pl.ds(0, LINE - 1)], sems.at[5])
    for r in range(2):
        for from_v in range(LINE):
            for half in range(2):
                rows = pl.ds(2 * from_v + half, 16, stride=16)
                delta = og[from_v, r, half * 16 : (half + 1) * 16].astype(F32)
                pnow[r, rows, :] = pair[r, rows, :] + delta * cnt[r, rows, :]

    lanes = lax.broadcasted_iota(jnp.int32, (1, S), 1)
    am = amino[...].astype(F32)
    for w in range(2):
        for r in range(2):
            x = norm(pnow[r], g_in[w : w + 1, :]).astype(BF16)
            here = jnp.sum(jnp.where(lanes == 2 * me + r, am, 0.0), axis=-1, keepdims=True)
            mask = am * here
            pt = dot_nt(wt[w], x)
            for side in range(2):
                at = side * 256
                val = jax.nn.sigmoid(pt[at + 128 : at + 256]) * pt[at : at + 128] * mask
                for j in range(2):
                    t32[pl.ds(side * 4 + r * 2 + j, 128, stride=8), :] = val[
                        :, j * 128 : (j + 1) * 128
                    ]
            tgate[r] = jax.nn.sigmoid(dot(x, wgate[w]))
        tsend[w] = t32[...].reshape(N, 8, 128).astype(BF16)
        trecv[w, me] = tsend[w, me]
        exchange(tsend.at[w], trecv.at[w], 6 + 2 * w)
        received(tsend.at[w], trecv.at[w], 6 + 2 * w)
        t32[...] = trecv[w].astype(F32).reshape(N * 8, 128)
        sides = []
        for side in range(2):
            sides.append(
                jnp.concatenate(
                    [
                        jnp.concatenate(
                            [
                                t32[pl.ds(side * 4 + r * 2 + j, 128, stride=8), :]
                                for j in range(2)
                            ],
                            axis=1,
                        )
                        for r in range(2)
                    ],
                    axis=0,
                )
            )
        if w == 0:
            prod = dot_nt(sides[0].astype(BF16), sides[1].astype(BF16))
        else:
            prod = dot(sides[0].T.astype(BF16), sides[1].astype(BF16))
        for j in range(2):
            xn[j] = prod[:, j * 128 : (j + 1) * 128]
        for r in range(2):
            for j in range(2):
                rows = pl.ds(r * 128, 128) if w == 0 else pl.ds(r, 128, stride=2)
                p32[pl.ds(r * 2 + j, 128, stride=4), :] = xn[j, rows, :]
        psend[w] = p32[...].reshape(N, 4, 128).astype(BF16)
        precv[w, me] = psend[w, me]
        exchange(psend.at[w], precv.at[w], 7 + 2 * w)
        received(psend.at[w], precv.at[w], 7 + 2 * w)
        p32[...] = precv[w].astype(F32).reshape(N * 4, 128)
        for r in range(2):
            for j in range(2):
                pn = norm(p32[pl.ds(r * 2 + j, 128, stride=4), :], gmt[w], axis=0)
                update = dot(pn.T.astype(BF16), wout[w])
                rows = pl.ds(j, 128, stride=2) if w == 0 else pl.ds(j * 128, 128)
                new = pnow[r, rows, :] + update * tgate[r, rows, :]
                if w == 0:
                    pnow[r, rows, :] = new
                else:
                    pair_out[r, rows, :] = new


def copied(a, b, a_out, b_out, sems):
    pltpu.make_async_copy(a, a_out, sems.at[0]).start()
    pltpu.make_async_copy(b, b_out, sems.at[1]).start()
    pltpu.make_async_copy(a, a_out, sems.at[0]).wait()
    pltpu.make_async_copy(b, b_out, sems.at[1]).wait()


SCRATCH = [
    ((BA, 128), BF16),
    ((BB, 128), BF16),
    ((2, N // 2, BA, 128), BF16),
    ((2, N // 2, BB, 128), BF16),
    ((N * BA, 128), F32),
    ((N * BB, 128), F32),
    ((2, S, 128), F32),
    ((2, 2, S, 128), F32),
    ((2, S, H), BF16),
    ((2, H, S), BF16),
    ((2, HEADS * S, H), BF16),
    ((2, S, HEADS * S), BF16),
    ((2, S, H), F32),
    ((N * 8, 128), F32),
    ((N, 8, 128), BF16),
    ((N, 8, 128), BF16),
    ((2, S, H), F32),
    ((S, S), F32),
    ((S, S), BF16),
    ((2, S, CZ), F32),
    ((2, 32, S), BF16),
    ((2, 32, S), BF16),
    ((LINE, 2, 32, S), BF16),
    ((2, PLANE, 32, S), BF16),
    ((2, 512, 128), F32),
    ((2, 512, S), BF16),
    ((128, 4096), BF16),
    ((4096, 512), BF16),
    ((LINE, 2, 32, 128), BF16),
    ((LINE, 2, 32, 128), BF16),
    ((2, 512, 128), BF16),
    ((2, CZ, CZ), F32),
    ((BA + BB, 128), F32),
    ((N * 8, 128), F32),
    ((2, N, 8, 128), BF16),
    ((2, N, 8, 128), BF16),
    ((2, S, CZ), F32),
    ((N * 4, 128), F32),
    ((2, N, 4, 128), BF16),
    ((2, N, 4, 128), BF16),
    ((2, S, CZ), F32),
]


def shards(*args):
    args = [a.reshape(1, -1) if a.ndim == 1 else a for a in args]
    for n in (9, 15):
        args[n] = args[n].T
    anywhere = pl.BlockSpec(memory_space=pl.ANY)
    local = pl.BlockSpec(memory_space=pltpu.VMEM)
    results = (
        jax.ShapeDtypeStruct((S * 4, 128), F32),
        jax.ShapeDtypeStruct((2, S, CZ), F32),
    )
    flat, pair = pl.pallas_call(
        body,
        out_shape=tuple(pltpu.VMEM(a.shape, a.dtype) for a in results),
        in_specs=[anywhere] * N_IN,
        out_specs=(local, local),
        scratch_shapes=[pltpu.VMEM(a.shape, a.dtype) for a in args]
        + [pltpu.VMEM(shape, dtype) for shape, dtype in SCRATCH]
        + [pltpu.SemaphoreType.DMA((n,)) for n in (13, 13, N_IN)],
        compiler_params=pltpu.CompilerParams(
            collective_id=0, has_side_effects=True, vmem_limit_bytes=60 << 20
        ),
    )(*args)
    flat, pair = pl.pallas_call(
        copied,
        out_shape=results,
        in_specs=[local] * 2,
        out_specs=(anywhere, anywhere),
        scratch_shapes=[pltpu.SemaphoreType.DMA((2,))],
    )(*(pltpu.with_memory_space_constraint(a, pltpu.VMEM) for a in (flat, pair)))
    return flat.reshape(S, 2, 2, 128).transpose(0, 2, 1, 3).reshape(S, 2, H), pair


def solution(mesh):
    rows = P("dap", None, None)
    return jax.shard_map(
        shards,
        mesh=mesh,
        in_specs=(rows, rows, P("dap", None)) + (P(),) * 19,
        out_specs=(P(None, "dap", None), rows),
        check_vma=False,
    )
```

```python
import math

import jax
import jax.numpy as jnp
from jax import lax
from jax.experimental import pallas as pl
from jax.experimental.pallas import tpu as pltpu
from jax.sharding import PartitionSpec as P

N = 128
S = 256
H = 256
CZ = 128
HEADS = 8
WIDTH = 32
PLANE = 16
LINE = 8
BA, BB, BC = 16, 16, 8
N_IN = 22
HOPS = (0, 1, 2, 1)
FAR_FIRST = sorted(
    [(a, b, c) for a in range(4) for b in range(4) for c in range(4)],
    key=lambda o: -(HOPS[o[0]] + HOPS[o[1]] + HOPS[o[2]]),
)
PLANE_FAR_FIRST = sorted(range(1, 16), key=lambda n: -(HOPS[n // 4] + HOPS[n % 4]))
EPS = 1e-05
PENALTY = 1e9
SCALE = 1.0 / math.sqrt(WIDTH)
F32, BF16 = jnp.float32, jnp.bfloat16
MESH = pl.DeviceIdType.MESH


def dot(a, b):
    return jnp.dot(a, b, preferred_element_type=F32)


def dot_nt(a, b):
    return lax.dot_general(a, b, (((1,), (1,)), ((), ())), preferred_element_type=F32)


def norm(x, gain, axis=-1):
    centred = x - jnp.mean(x, axis=axis, keepdims=True)
    spread = jnp.mean(centred * centred, axis=axis, keepdims=True)
    return centred * lax.rsqrt(spread + EPS) * gain


def send(src, dst, ssem, rsem, to):
    pltpu.make_async_remote_copy(
        src_ref=src, dst_ref=dst, send_sem=ssem, recv_sem=rsem, device_id=(to,), device_id_type=MESH
    ).start()


def landed(like, sem):
    pltpu.make_async_copy(like, like, sem).wait()


def every_other(halves, first):
    return jnp.concatenate([halves[c, pl.ds(first, 128, stride=2), :] for c in range(2)], axis=1)


def head_lanes(h):
    lanes = lax.broadcasted_iota(jnp.int32, (1, H), 1)
    return jnp.logical_and(lanes >= h * WIDTH, lanes < (h + 1) * WIDTH).astype(F32).astype(BF16)


def spread_heads(v, vbd, t):
    for h in range(HEADS):
        vbd[t, h * S : (h + 1) * S, :] = v * head_lanes(h)


def probabilities(scores):
    top = jnp.max(scores, axis=-1, keepdims=True)
    e = jnp.exp(scores - top)
    return (e * (1.0 / jnp.sum(e, axis=-1, keepdims=True))).astype(BF16)


def body(*refs):
    ins, outs, refs = refs[:N_IN], refs[N_IN : N_IN + 2], refs[N_IN + 2 :]
    here, refs = refs[:N_IN], refs[N_IN:]
    msa_out, pair_out = outs
    (
        msa, pair, pres, amino, g_row, wq1, wkvg1, wo1, g_bias, wb, g_col,
        wq2, wkvg2, wo2, g_opm, wlr, wfin, g_in, wproj, wgate, g_mid, wout,
    ) = here
    (
        bsa, bsb, bsc, ba, bb, bc, wa, wb32, wc, raw, tx, xn, msah, q, kt, vbd, prob, gate, a32,
        asend, arecv, xc, pm, pmt, cnt, lsend, rsend, lg, rg, r32, rp, lhs2, bd, osend, og,
        wt, gmt, pad, t32, tsend, trecv, tgate, p32, psend, precv, pnow,
        ssem, rsem, isem,
    ) = refs
    me = lax.axis_index("dap")
    core = lax.rem(me, 2)
    partner = me + 1 - 2 * core
    chip = me // 2
    my_u, my_v = me // LINE, lax.rem(me, LINE)

    x_at, y_at, z_at = me // 32, lax.rem(me // 8, 4), lax.rem(chip, 4)

    def chips():
        for a, b, c in FAR_FIRST:
            yield (
                lax.rem(x_at + a, 4) * 16 + lax.rem(y_at + b, 4) * 4 + lax.rem(z_at + c, 4),
                (a, b, c) == (0, 0, 0),
            )

    def peers():
        for there, here in chips():
            if not here:
                yield there * 2 + core
            yield there * 2 + 1 - core

    def plane():
        for n in PLANE_FAR_FIRST:
            yield lax.rem(x_at + n // 4, 4) * 4 + lax.rem(y_at + n % 4, 4)

    def line():
        for n in (2, 1, 3, 0):
            if n:
                yield lax.rem(z_at + n, 4) * 2 + core
            yield lax.rem(z_at + n, 4) * 2 + 1 - core

    barrier = pltpu.get_barrier_semaphore()
    for to in peers():
        pl.semaphore_signal(barrier, inc=1, device_id=(to,), device_id_type=MESH)

    order = (1, 8, 9, 2, 0, 4, 5, 6, 18, 20, 16, 7, 3, 10, 11, 12, 13, 14, 15, 17, 19, 21)
    for n in order:
        pltpu.make_async_copy(ins[n], here[n], isem.at[n]).start()

    def arrived(*which):
        for n in which:
            pltpu.make_async_copy(ins[n], here[n], isem.at[n]).wait()

    arrived(1, 8, 9, 2)
    wbt = wb[...]
    pad[...] = jnp.zeros_like(pad)
    for r in range(2):
        pn = norm(pair[r], g_bias[...]).astype(BF16)
        bt = dot_nt(wbt, pn)
        for j in range(2):
            cols = slice(j * 128, (j + 1) * 128)
            at = (r * 2 + j) * 4
            pad[at : at + 4, :] = bt[0:4, cols]
            pad[BA + at : BA + at + 4, :] = bt[4:8, cols]
    presence = pres[...].astype(F32)
    for r in range(2):
        for j in range(2):
            at = BA + BB + r * 2 + j
            pad[at : at + 1, :] = presence[r : r + 1, j * 128 : (j + 1) * 128]
    bsa[...] = pad[0:BA, :].astype(BF16)
    bsb[...] = pad[BA : BA + BB, :].astype(BF16)
    bsc[...] = pad[BA + BB :, :].astype(BF16)
    ba[core, chip] = bsa[...]
    bb[core, chip] = bsb[...]
    bc[core, chip] = bsc[...]

    arrived(0, 4, 5, 6)
    for s in range(2):
        x = norm(msa[s], g_row[...])
        for c in range(2):
            xn[c] = x[:, c * 128 : (c + 1) * 128]
            msah[s, c] = msa[s, :, c * 128 : (c + 1) * 128]
        xb = x.astype(BF16)
        kt[s] = dot(xb, wkvg1[:, 0:H]).T.astype(BF16)
        spread_heads(dot(xb, wkvg1[:, H : 2 * H]).astype(BF16), vbd, s)
        for r in range(2):
            rows = slice(r * 128, (r + 1) * 128)
            xr = every_other(xn, r).astype(BF16)
            q[s, rows] = (dot(xr, wq1[...]) * SCALE).astype(BF16)
            gate[s, rows] = jax.nn.sigmoid(dot(xr, wkvg1[:, 2 * H :]))

    arrived(18, 20, 16, 7, 3, 10, 11, 12, 13, 14, 15, 17, 19, 21)
    for w in range(2):
        for c in range(4):
            cols = slice(c * 128, (c + 1) * 128)
            wt[w, cols, :] = wproj[w, :, cols].astype(F32).T.astype(BF16)
        gmt[w] = jnp.broadcast_to(g_mid[w : w + 1, :], (CZ, CZ)).T
    p32[...] = wfin[0:512, :].astype(F32)
    t32[0:512, :] = wfin[512:1024, :].astype(F32)
    bd[...] = jnp.zeros_like(bd)
    for b in range(32):
        part = jnp.concatenate(
            [p32[pl.ds(b, 16, stride=32), :], t32[pl.ds(b, 16, stride=32), :]], axis=0
        ).astype(BF16)
        for i in range(4):
            bd[b * 128 + i * 32 : b * 128 + (i + 1) * 32, i * 128 : (i + 1) * 128] = part

    pl.semaphore_wait(barrier, N - 1)
    for src, dst, sem in ((bsa, ba, 0), (bsb, bb, 10), (bsc, bc, 13)):
        for there, here in chips():
            if not here:
                send(src, dst.at[core, chip], ssem.at[sem], rsem.at[sem], there * 2 + core)

    pens = [PENALTY * (presence[s : s + 1, :] - 1.0) for s in range(2)]
    for h in range(HEADS):
        for t in range(2):
            raw[t, :, h * S : (h + 1) * S] = dot(q[t] * head_lanes(h), kt[t])

    halves = ((ba, wa, BA, 0), (bb, wb32, BB, 10))

    sent = []

    def swap(dst, sem):
        landed(dst.at[0, pl.ds(0, N // 2 - 1)], rsem.at[sem])
        send(dst.at[core], dst.at[core], ssem.at[sem + 1], rsem.at[sem + 1], partner)

    def swapped(dst, wide, rows_of, sem):
        landed(dst.at[0], rsem.at[sem + 1])
        sent.append((dst.at[0, pl.ds(0, N // 2 - 1)], sem))
        sent.append((dst.at[0], sem + 1))
        for d in range(N):
            wide[d * rows_of : (d + 1) * rows_of, :] = dst[d % 2, d // 2].astype(F32)

    swap(ba, 0)
    for half, (dst, wide, rows_of, sem) in enumerate(halves):
        swapped(dst, wide, rows_of, sem)
        for h in range(4):
            bias = jnp.concatenate(
                [
                    jnp.concatenate(
                        [
                            wide[pl.ds((r * 2 + j) * 4 + h, 128, stride=rows_of), :]
                            for j in range(2)
                        ],
                        axis=1,
                    )
                    for r in range(2)
                ],
                axis=0,
            )
            for t in range(2):
                at = slice((half * 4 + h) * S, (half * 4 + h + 1) * S)
                prob[t, :, at] = probabilities(raw[t, :, at] + bias + pens[t])
            if half == 0 and h == 1:
                swap(bb, 10)
    swap(bc, 13)
    for s in range(2):
        y = (dot(prob[s], vbd[s]) * gate[s]).astype(BF16)
        step = dot(y, wo1[...])
        for r in range(2):
            one = every_other(msah.at[s], r) + step[r * 128 : (r + 1) * 128]
            for c in range(2):
                a32[pl.ds((s * 2 + r) * 2 + c, 128, stride=8), :] = one[:, c * 128 : (c + 1) * 128]
    asend[...] = a32[...].reshape(N, 8, 128).astype(BF16)
    arecv[me] = asend[me]

    def exchange(src, dst, sem):
        for to in peers():
            send(src.at[to], dst.at[me], ssem.at[sem], rsem.at[sem], to)

    def received(src, dst, sem):
        landed(dst.at[pl.ds(0, N - 1)], rsem.at[sem])
        sent.append((src.at[pl.ds(0, N - 1)], sem))

    exchange(asend, arecv, 2)

    swapped(bc, wc, BC, 13)
    for s in range(2):
        for j in range(2):
            pm[s * 128 : (s + 1) * 128, j * 128 : (j + 1) * 128] = wc[
                pl.ds(s * 2 + j, 128, stride=BC), :
            ]
    pmt[...] = pm[...].T.astype(BF16)
    own = lax.broadcasted_iota(jnp.int32, (16, S), 0) + 2 * me
    hot = (lax.broadcasted_iota(jnp.int32, (16, S), 1) == own).astype(F32).astype(BF16)
    mine = dot(hot, pmt[...])
    pmb = pm[...].astype(BF16)
    for r in range(2):
        hot_c = (lax.broadcasted_iota(jnp.int32, (S, 128), 0) == 2 * me + r).astype(F32)
        col = dot(pmb, hot_c.astype(BF16)).astype(BF16)
        cnt[r] = 1.0 / jnp.maximum(dot(pmt[...], col), 1.0)

    received(asend, arecv, 2)
    a32[...] = arecv[...].astype(F32).reshape(N * 8, 128)
    for r in range(2):
        for s in range(2):
            for c in range(2):
                xc[r, s * 128 : (s + 1) * 128, c * 128 : (c + 1) * 128] = a32[
                    pl.ds((s * 2 + r) * 2 + c, 128, stride=8), :
                ]
        xb = norm(xc[r], g_col[...]).astype(BF16)
        q[r] = (dot(xb, wq2[...]) * SCALE).astype(BF16)
        kt[r] = dot(xb, wkvg2[:, 0:H]).T.astype(BF16)
        spread_heads(dot(xb, wkvg2[:, H : 2 * H]).astype(BF16), vbd, r)
        gate[r] = jax.nn.sigmoid(dot(xb, wkvg2[:, 2 * H :]))
    for r in range(2):
        for h in range(HEADS):
            scores = dot(q[r] * head_lanes(h), kt[r]) + PENALTY * (mine[r : r + 1, :] - 1.0)
            prob[r, :, h * S : (h + 1) * S] = probabilities(scores)
        y = (dot(prob[r], vbd[r]) * gate[r]).astype(BF16)
        done = xc[r] + dot(y, wo2[...])
        xb = norm(done, g_opm[...]).astype(BF16)
        projected = dot_nt(wlr[...], xb) * mine[r : r + 1, :]
        lsend[r] = projected[0:32].astype(BF16)
        rsend[r] = projected[32:64].astype(BF16)
        rg[r, my_u] = rsend[r]
        if r == 1:
            lg[my_v] = lsend[...]
            for to_v in line():
                send(lsend, lg.at[my_v], ssem.at[4], rsem.at[4], my_u * LINE + to_v)
        for to_u in plane():
            to = to_u * LINE + my_v
            send(rsend.at[r], rg.at[r, my_u], ssem.at[3 + 9 * r], rsem.at[3 + 9 * r], to)
        for s in range(2):
            for c in range(2):
                msa_out[pl.ds(s * 4 + c * 2 + r, 128, stride=8), :] = done[
                    s * 128 : (s + 1) * 128, c * 128 : (c + 1) * 128
                ]

    for r in range(2):
        landed(rg.at[0, pl.ds(0, PLANE - 1)], rsem.at[3 + 9 * r])
        sent.append((rg.at[0, pl.ds(0, PLANE - 1)], 3 + 9 * r))
        for c in range(2):
            r32[c] = rg[r, :, :, c * 128 : (c + 1) * 128].astype(F32).reshape(512, 128)
        for b in range(32):
            rp[r, b * 16 : (b + 1) * 16, :] = jnp.concatenate(
                [r32[c, pl.ds(b, 16, stride=32), :] for c in range(2)], axis=1
            ).astype(BF16)
        if r == 0:
            landed(lg.at[pl.ds(0, LINE - 1)], rsem.at[4])
            sent.append((lg.at[pl.ds(0, LINE - 1)], 4))
        for g in range(4):
            lb = lg[2 * g : 2 * g + 2].reshape(128, S)
            u = dot_nt(rp[r], lb).astype(BF16)
            at = g * 32 + r * 16
            for b in range(32):
                lhs2[at : at + 16, b * 128 : (b + 1) * 128] = u[b * 16 : (b + 1) * 16]
    block = dot(lhs2[...], bd[...])
    for to_v in range(LINE):
        for r in range(2):
            row, at = (to_v // 2) * 32, (to_v % 2) * 2 + r
            osend[to_v, r] = block[row : row + 32, at * 128 : (at + 1) * 128].astype(BF16)
    og[my_v] = osend[my_v]
    for to_v in line():
        send(osend.at[to_v], og.at[my_v], ssem.at[5], rsem.at[5], my_u * LINE + to_v)
    landed(og.at[pl.ds(0, LINE - 1)], rsem.at[5])
    sent.append((og.at[pl.ds(0, LINE - 1)], 5))
    for r in range(2):
        for from_v in range(LINE):
            for half in range(2):
                rows = pl.ds(2 * from_v + half, 16, stride=16)
                delta = og[from_v, r, half * 16 : (half + 1) * 16].astype(F32)
                pnow[r, rows, :] = pair[r, rows, :] + delta * cnt[r, rows, :]

    lanes = lax.broadcasted_iota(jnp.int32, (1, S), 1)
    am = amino[...].astype(F32)
    for w in range(2):
        for r in range(2):
            x = norm(pnow[r], g_in[w : w + 1, :]).astype(BF16)
            here = jnp.sum(jnp.where(lanes == 2 * me + r, am, 0.0), axis=-1, keepdims=True)
            mask = am * here
            pt = dot_nt(wt[w], x)
            for side in range(2):
                at = side * 256
                val = jax.nn.sigmoid(pt[at + 128 : at + 256]) * pt[at : at + 128] * mask
                for j in range(2):
                    t32[pl.ds(side * 4 + r * 2 + j, 128, stride=8), :] = val[
                        :, j * 128 : (j + 1) * 128
                    ]
            tx[r] = x
        tsend[w] = t32[...].reshape(N, 8, 128).astype(BF16)
        trecv[w, me] = tsend[w, me]
        exchange(tsend.at[w], trecv.at[w], 6 + 2 * w)
        for r in range(2):
            tgate[r] = jax.nn.sigmoid(dot(tx[r], wgate[w]))
        received(tsend.at[w], trecv.at[w], 6 + 2 * w)
        t32[...] = trecv[w].astype(F32).reshape(N * 8, 128)
        sides = []
        for side in range(2):
            sides.append(
                jnp.concatenate(
                    [
                        jnp.concatenate(
                            [
                                t32[pl.ds(side * 4 + r * 2 + j, 128, stride=8), :]
                                for j in range(2)
                            ],
                            axis=1,
                        )
                        for r in range(2)
                    ],
                    axis=0,
                )
            )
        if w == 0:
            prod = dot_nt(sides[0].astype(BF16), sides[1].astype(BF16))
        else:
            prod = dot(sides[0].T.astype(BF16), sides[1].astype(BF16))
        for j in range(2):
            xn[j] = prod[:, j * 128 : (j + 1) * 128]
        for r in range(2):
            for j in range(2):
                rows = pl.ds(r * 128, 128) if w == 0 else pl.ds(r, 128, stride=2)
                p32[pl.ds(r * 2 + j, 128, stride=4), :] = xn[j, rows, :]
        psend[w] = p32[...].reshape(N, 4, 128).astype(BF16)
        precv[w, me] = psend[w, me]
        exchange(psend.at[w], precv.at[w], 7 + 2 * w)
        received(psend.at[w], precv.at[w], 7 + 2 * w)
        p32[...] = precv[w].astype(F32).reshape(N * 4, 128)
        for r in range(2):
            for j in range(2):
                pn = norm(p32[pl.ds(r * 2 + j, 128, stride=4), :], gmt[w], axis=0)
                update = dot(pn.T.astype(BF16), wout[w])
                rows = pl.ds(j, 128, stride=2) if w == 0 else pl.ds(j * 128, 128)
                new = pnow[r, rows, :] + update * tgate[r, rows, :]
                if w == 0:
                    pnow[r, rows, :] = new
                else:
                    pair_out[r, rows, :] = new

    for like, sem in sent:
        landed(like, ssem.at[sem])


def copied(a, b, a_out, b_out, sems):
    pltpu.make_async_copy(a, a_out, sems.at[0]).start()
    pltpu.make_async_copy(b, b_out, sems.at[1]).start()
    pltpu.make_async_copy(a, a_out, sems.at[0]).wait()
    pltpu.make_async_copy(b, b_out, sems.at[1]).wait()


SCRATCH = [
    ((BA, 128), BF16),
    ((BB, 128), BF16),
    ((BC, 128), BF16),
    ((2, N // 2, BA, 128), BF16),
    ((2, N // 2, BB, 128), BF16),
    ((2, N // 2, BC, 128), BF16),
    ((N * BA, 128), F32),
    ((N * BB, 128), F32),
    ((N * BC, 128), F32),
    ((2, S, HEADS * S), F32),
    ((2, S, CZ), BF16),
    ((2, S, 128), F32),
    ((2, 2, S, 128), F32),
    ((2, S, H), BF16),
    ((2, H, S), BF16),
    ((2, HEADS * S, H), BF16),
    ((2, S, HEADS * S), BF16),
    ((2, S, H), F32),
    ((N * 8, 128), F32),
    ((N, 8, 128), BF16),
    ((N, 8, 128), BF16),
    ((2, S, H), F32),
    ((S, S), F32),
    ((S, S), BF16),
    ((2, S, CZ), F32),
    ((2, 32, S), BF16),
    ((2, 32, S), BF16),
    ((LINE, 2, 32, S), BF16),
    ((2, PLANE, 32, S), BF16),
    ((2, 512, 128), F32),
    ((2, 512, S), BF16),
    ((128, 4096), BF16),
    ((4096, 512), BF16),
    ((LINE, 2, 32, 128), BF16),
    ((LINE, 2, 32, 128), BF16),
    ((2, 512, 128), BF16),
    ((2, CZ, CZ), F32),
    ((BA + BB + BC, 128), F32),
    ((N * 8, 128), F32),
    ((2, N, 8, 128), BF16),
    ((2, N, 8, 128), BF16),
    ((2, S, CZ), F32),
    ((N * 4, 128), F32),
    ((2, N, 4, 128), BF16),
    ((2, N, 4, 128), BF16),
    ((2, S, CZ), F32),
]


def shards(*args):
    args = [a.reshape(1, -1) if a.ndim == 1 else a for a in args]
    for n in (9, 15):
        args[n] = args[n].T
    anywhere = pl.BlockSpec(memory_space=pl.ANY)
    local = pl.BlockSpec(memory_space=pltpu.VMEM)
    results = (
        jax.ShapeDtypeStruct((S * 4, 128), F32),
        jax.ShapeDtypeStruct((2, S, CZ), F32),
    )
    flat, pair = pl.pallas_call(
        body,
        out_shape=tuple(pltpu.VMEM(a.shape, a.dtype) for a in results),
        in_specs=[anywhere] * N_IN,
        out_specs=(local, local),
        scratch_shapes=[pltpu.VMEM(a.shape, a.dtype) for a in args]
        + [pltpu.VMEM(shape, dtype) for shape, dtype in SCRATCH]
        + [pltpu.SemaphoreType.DMA((n,)) for n in (15, 15, N_IN)],
        compiler_params=pltpu.CompilerParams(
            collective_id=0, has_side_effects=True, vmem_limit_bytes=60 << 20
        ),
    )(*args)
    flat, pair = pl.pallas_call(
        copied,
        out_shape=results,
        in_specs=[local] * 2,
        out_specs=(anywhere, anywhere),
        scratch_shapes=[pltpu.SemaphoreType.DMA((2,))],
    )(*(pltpu.with_memory_space_constraint(a, pltpu.VMEM) for a in (flat, pair)))
    return flat.reshape(S, 2, 2, 128).transpose(0, 2, 1, 3).reshape(S, 2, H), pair


def solution(mesh):
    rows = P("dap", None, None)
    return jax.shard_map(
        shards,
        mesh=mesh,
        in_specs=(rows, rows, P("dap", None)) + (P(),) * 19,
        out_specs=(P(None, "dap", None), rows),
        check_vma=False,
    )
```

```python
import math

import jax
import jax.numpy as jnp
from jax import lax
from jax.experimental import pallas as pl
from jax.experimental.pallas import tpu as pltpu
from jax.sharding import PartitionSpec as P

N = 128
S = 256
H = 256
CZ = 128
HEADS = 8
WIDTH = 32
PLANE = 16
LINE = 8
BA, BB, BC = 16, 16, 8
N_IN = 22
HOPS = (0, 1, 2, 1)
FAR_FIRST = sorted(
    [(a, b, c) for a in range(4) for b in range(4) for c in range(4)],
    key=lambda o: -(HOPS[o[0]] + HOPS[o[1]] + HOPS[o[2]]),
)
PLANE_FAR_FIRST = sorted(range(1, 16), key=lambda n: -(HOPS[n // 4] + HOPS[n % 4]))
EPS = 1e-05
PENALTY = 1e9
SCALE = 1.0 / math.sqrt(WIDTH)
F32, BF16 = jnp.float32, jnp.bfloat16
MESH = pl.DeviceIdType.MESH


def dot(a, b):
    return jnp.dot(a, b, preferred_element_type=F32)


def dot_nt(a, b):
    return lax.dot_general(a, b, (((1,), (1,)), ((), ())), preferred_element_type=F32)


def norm(x, gain, axis=-1):
    centred = x - jnp.mean(x, axis=axis, keepdims=True)
    spread = jnp.mean(centred * centred, axis=axis, keepdims=True)
    return centred * lax.rsqrt(spread + EPS) * gain


def send(src, dst, ssem, rsem, to):
    pltpu.make_async_remote_copy(
        src_ref=src, dst_ref=dst, send_sem=ssem, recv_sem=rsem, device_id=(to,), device_id_type=MESH
    ).start()


def landed(like, sem):
    pltpu.make_async_copy(like, like, sem).wait()


def every_other(halves, first):
    return jnp.concatenate([halves[c, pl.ds(first, 128, stride=2), :] for c in range(2)], axis=1)


def head_lanes(h):
    lanes = lax.broadcasted_iota(jnp.int32, (1, H), 1)
    return jnp.logical_and(lanes >= h * WIDTH, lanes < (h + 1) * WIDTH).astype(F32).astype(BF16)


def spread_heads(v, vbd, t):
    for h in range(HEADS):
        vbd[t, h * S : (h + 1) * S, :] = v * head_lanes(h)


def probabilities(scores):
    top = jnp.max(scores, axis=-1, keepdims=True)
    e = jnp.exp(scores - top)
    return (e * (1.0 / jnp.sum(e, axis=-1, keepdims=True))).astype(BF16)


def body(*refs):
    ins, outs, refs = refs[:N_IN], refs[N_IN : N_IN + 2], refs[N_IN + 2 :]
    here, refs = refs[:N_IN], refs[N_IN:]
    msa_out, pair_out = outs
    (
        msa, pair, pres, amino, g_row, wq1, wkvg1, wo1, g_bias, wb, g_col,
        wq2, wkvg2, wo2, g_opm, wlr, wfin, g_in, wproj, wgate, g_mid, wout,
    ) = here
    (
        bsa, bsb, bsc, ba, bb, bc, wa, wb32, wc, raw, tx, xn, msah, q, kt, vbd, prob, gate, a32,
        asend, arecv, xc, pm, pmt, cnt, lsend, rsend, lg, rg, r32, rp, lhs2, bd, osend, og,
        wt, gmt, pad, t32, tsend, trecv, tgate, p32, psend, precv, pnow,
        ssem, rsem, isem,
    ) = refs
    me = lax.axis_index("dap")
    core = lax.rem(me, 2)
    partner = me + 1 - 2 * core
    chip = me // 2
    my_u, my_v = me // LINE, lax.rem(me, LINE)

    x_at, y_at, z_at = me // 32, lax.rem(me // 8, 4), lax.rem(chip, 4)

    def chips():
        for a, b, c in FAR_FIRST:
            yield (
                lax.rem(x_at + a, 4) * 16 + lax.rem(y_at + b, 4) * 4 + lax.rem(z_at + c, 4),
                (a, b, c) == (0, 0, 0),
            )

    def peers():
        for there, here in chips():
            if not here:
                yield there * 2 + core
            yield there * 2 + 1 - core

    def plane():
        for n in PLANE_FAR_FIRST:
            yield lax.rem(x_at + n // 4, 4) * 4 + lax.rem(y_at + n % 4, 4)

    def line():
        for n in (2, 1, 3, 0):
            if n:
                yield lax.rem(z_at + n, 4) * 2 + core
            yield lax.rem(z_at + n, 4) * 2 + 1 - core

    barrier = pltpu.get_barrier_semaphore()
    for to in peers():
        pl.semaphore_signal(barrier, inc=1, device_id=(to,), device_id_type=MESH)

    order = (1, 8, 9, 2, 0, 4, 5, 6, 18, 20, 16, 7, 3, 10, 11, 12, 13, 14, 15, 17, 19, 21)
    for n in order:
        pltpu.make_async_copy(ins[n], here[n], isem.at[n]).start()

    def arrived(*which):
        for n in which:
            pltpu.make_async_copy(ins[n], here[n], isem.at[n]).wait()

    arrived(1, 8, 9, 2)
    wbt = wb[...]
    pad[...] = jnp.zeros_like(pad)
    for r in range(2):
        pn = norm(pair[r], g_bias[...]).astype(BF16)
        bt = dot_nt(wbt, pn)
        for j in range(2):
            cols = slice(j * 128, (j + 1) * 128)
            at = (r * 2 + j) * 4
            pad[at : at + 4, :] = bt[0:4, cols]
            pad[BA + at : BA + at + 4, :] = bt[4:8, cols]
    presence = pres[...].astype(F32)
    for r in range(2):
        for j in range(2):
            at = BA + BB + r * 2 + j
            pad[at : at + 1, :] = presence[r : r + 1, j * 128 : (j + 1) * 128]
    bsa[...] = pad[0:BA, :].astype(BF16)
    bsb[...] = pad[BA : BA + BB, :].astype(BF16)
    bsc[...] = pad[BA + BB :, :].astype(BF16)
    ba[core, chip] = bsa[...]
    bb[core, chip] = bsb[...]
    bc[core, chip] = bsc[...]

    arrived(0, 4, 5, 6)
    for s in range(2):
        x = norm(msa[s], g_row[...])
        for c in range(2):
            xn[c] = x[:, c * 128 : (c + 1) * 128]
            msah[s, c] = msa[s, :, c * 128 : (c + 1) * 128]
        xb = x.astype(BF16)
        kt[s] = dot(xb, wkvg1[:, 0:H]).T.astype(BF16)
        spread_heads(dot(xb, wkvg1[:, H : 2 * H]).astype(BF16), vbd, s)
        for r in range(2):
            rows = slice(r * 128, (r + 1) * 128)
            xr = every_other(xn, r).astype(BF16)
            q[s, rows] = (dot(xr, wq1[...]) * SCALE).astype(BF16)
            gate[s, rows] = jax.nn.sigmoid(dot(xr, wkvg1[:, 2 * H :]))

    arrived(18, 20, 16, 7, 3, 10, 11, 12, 13, 14, 15, 17, 19, 21)
    for w in range(2):
        for c in range(4):
            cols = slice(c * 128, (c + 1) * 128)
            wt[w, cols, :] = wproj[w, :, cols].astype(F32).T.astype(BF16)
        gmt[w] = jnp.broadcast_to(g_mid[w : w + 1, :], (CZ, CZ)).T
    p32[...] = wfin[0:512, :].astype(F32)
    t32[0:512, :] = wfin[512:1024, :].astype(F32)
    bd[...] = jnp.zeros_like(bd)
    for b in range(32):
        part = jnp.concatenate(
            [p32[pl.ds(b, 16, stride=32), :], t32[pl.ds(b, 16, stride=32), :]], axis=0
        ).astype(BF16)
        for i in range(4):
            bd[b * 128 + i * 32 : b * 128 + (i + 1) * 32, i * 128 : (i + 1) * 128] = part

    pl.semaphore_wait(barrier, N - 1)
    for src, dst, sem in ((bsa, ba, 0), (bsb, bb, 10), (bsc, bc, 13)):
        for there, here in chips():
            if not here:
                send(src, dst.at[core, chip], ssem.at[sem], rsem.at[sem], there * 2 + core)

    pens = [PENALTY * (presence[s : s + 1, :] - 1.0) for s in range(2)]
    for h in range(HEADS):
        for t in range(2):
            raw[t, :, h * S : (h + 1) * S] = dot(q[t] * head_lanes(h), kt[t])

    halves = ((ba, wa, BA, 0), (bb, wb32, BB, 10))

    sent = []

    def swap(dst, sem):
        landed(dst.at[0, pl.ds(0, N // 2 - 1)], rsem.at[sem])
        send(dst.at[core], dst.at[core], ssem.at[sem + 1], rsem.at[sem + 1], partner)

    def swapped(dst, wide, rows_of, sem):
        landed(dst.at[0], rsem.at[sem + 1])
        sent.append((dst.at[0, pl.ds(0, N // 2 - 1)], sem))
        sent.append((dst.at[0], sem + 1))
        for d in range(N):
            wide[d * rows_of : (d + 1) * rows_of, :] = dst[d % 2, d // 2].astype(F32)

    swap(ba, 0)
    for half, (dst, wide, rows_of, sem) in enumerate(halves):
        swapped(dst, wide, rows_of, sem)
        for h in range(4):
            bias = jnp.concatenate(
                [
                    jnp.concatenate(
                        [
                            wide[pl.ds((r * 2 + j) * 4 + h, 128, stride=rows_of), :]
                            for j in range(2)
                        ],
                        axis=1,
                    )
                    for r in range(2)
                ],
                axis=0,
            )
            for t in range(2):
                at = slice((half * 4 + h) * S, (half * 4 + h + 1) * S)
                prob[t, :, at] = probabilities(raw[t, :, at] + bias + pens[t])
            if half == 0 and h == 1:
                swap(bb, 10)
    swap(bc, 13)
    for s in range(2):
        y = (dot(prob[s], vbd[s]) * gate[s]).astype(BF16)
        step = dot(y, wo1[...])
        for r in range(2):
            one = every_other(msah.at[s], r) + step[r * 128 : (r + 1) * 128]
            for c in range(2):
                a32[pl.ds((s * 2 + r) * 2 + c, 128, stride=8), :] = one[:, c * 128 : (c + 1) * 128]
    asend[...] = a32[...].reshape(N, 8, 128).astype(BF16)
    arecv[me] = asend[me]

    def exchange(src, dst, sem):
        for to in peers():
            send(src.at[to], dst.at[me], ssem.at[sem], rsem.at[sem], to)

    def received(src, dst, sem):
        landed(dst.at[pl.ds(0, N - 1)], rsem.at[sem])
        sent.append((src.at[pl.ds(0, N - 1)], sem))

    exchange(asend, arecv, 2)

    swapped(bc, wc, BC, 13)
    for s in range(2):
        for j in range(2):
            pm[s * 128 : (s + 1) * 128, j * 128 : (j + 1) * 128] = wc[
                pl.ds(s * 2 + j, 128, stride=BC), :
            ]
    pmt[...] = pm[...].T.astype(BF16)
    own = lax.broadcasted_iota(jnp.int32, (16, S), 0) + 2 * me
    hot = (lax.broadcasted_iota(jnp.int32, (16, S), 1) == own).astype(F32).astype(BF16)
    mine = dot(hot, pmt[...])
    pmb = pm[...].astype(BF16)
    for r in range(2):
        hot_c = (lax.broadcasted_iota(jnp.int32, (S, 128), 0) == 2 * me + r).astype(F32)
        col = dot(pmb, hot_c.astype(BF16)).astype(BF16)
        cnt[r] = 1.0 / jnp.maximum(dot(pmt[...], col), 1.0)

    received(asend, arecv, 2)
    a32[...] = arecv[...].astype(F32).reshape(N * 8, 128)
    for r in range(2):
        for s in range(2):
            for c in range(2):
                xc[r, s * 128 : (s + 1) * 128, c * 128 : (c + 1) * 128] = a32[
                    pl.ds((s * 2 + r) * 2 + c, 128, stride=8), :
                ]
        xb = norm(xc[r], g_col[...]).astype(BF16)
        q[r] = (dot(xb, wq2[...]) * SCALE).astype(BF16)
        kt[r] = dot(xb, wkvg2[:, 0:H]).T.astype(BF16)
        spread_heads(dot(xb, wkvg2[:, H : 2 * H]).astype(BF16), vbd, r)
        gate[r] = jax.nn.sigmoid(dot(xb, wkvg2[:, 2 * H :]))
        for h in range(HEADS):
            scores = dot(q[r] * head_lanes(h), kt[r]) + PENALTY * (mine[r : r + 1, :] - 1.0)
            prob[r, :, h * S : (h + 1) * S] = probabilities(scores)
        y = (dot(prob[r], vbd[r]) * gate[r]).astype(BF16)
        done = xc[r] + dot(y, wo2[...])
        xb = norm(done, g_opm[...]).astype(BF16)
        projected = dot_nt(wlr[...], xb) * mine[r : r + 1, :]
        lsend[r] = projected[0:32].astype(BF16)
        rsend[r] = projected[32:64].astype(BF16)
        rg[r, my_u] = rsend[r]
        if r == 1:
            lg[my_v] = lsend[...]
            for to_v in line():
                send(lsend, lg.at[my_v], ssem.at[4], rsem.at[4], my_u * LINE + to_v)
        for to_u in plane():
            to = to_u * LINE + my_v
            send(rsend.at[r], rg.at[r, my_u], ssem.at[3 + 9 * r], rsem.at[3 + 9 * r], to)
        for s in range(2):
            for c in range(2):
                msa_out[pl.ds(s * 4 + c * 2 + r, 128, stride=8), :] = done[
                    s * 128 : (s + 1) * 128, c * 128 : (c + 1) * 128
                ]

    for r in range(2):
        landed(rg.at[0, pl.ds(0, PLANE - 1)], rsem.at[3 + 9 * r])
        sent.append((rg.at[0, pl.ds(0, PLANE - 1)], 3 + 9 * r))
        for c in range(2):
            r32[c] = rg[r, :, :, c * 128 : (c + 1) * 128].astype(F32).reshape(512, 128)
        for b in range(32):
            rp[r, b * 16 : (b + 1) * 16, :] = jnp.concatenate(
                [r32[c, pl.ds(b, 16, stride=32), :] for c in range(2)], axis=1
            ).astype(BF16)
        if r == 0:
            landed(lg.at[pl.ds(0, LINE - 1)], rsem.at[4])
            sent.append((lg.at[pl.ds(0, LINE - 1)], 4))
        for g in range(4):
            lb = lg[2 * g : 2 * g + 2].reshape(128, S)
            u = dot_nt(rp[r], lb).astype(BF16)
            at = g * 32 + r * 16
            for b in range(32):
                lhs2[at : at + 16, b * 128 : (b + 1) * 128] = u[b * 16 : (b + 1) * 16]
    block = dot(lhs2[...], bd[...])
    for to_v in range(LINE):
        for r in range(2):
            row, at = (to_v // 2) * 32, (to_v % 2) * 2 + r
            osend[to_v, r] = block[row : row + 32, at * 128 : (at + 1) * 128].astype(BF16)
    og[my_v] = osend[my_v]
    for to_v in line():
        send(osend.at[to_v], og.at[my_v], ssem.at[5], rsem.at[5], my_u * LINE + to_v)
    landed(og.at[pl.ds(0, LINE - 1)], rsem.at[5])
    sent.append((og.at[pl.ds(0, LINE - 1)], 5))
    for r in range(2):
        for from_v in range(LINE):
            for half in range(2):
                rows = pl.ds(2 * from_v + half, 16, stride=16)
                delta = og[from_v, r, half * 16 : (half + 1) * 16].astype(F32)
                pnow[r, rows, :] = pair[r, rows, :] + delta * cnt[r, rows, :]

    lanes = lax.broadcasted_iota(jnp.int32, (1, S), 1)
    am = amino[...].astype(F32)
    for w in range(2):
        for r in range(2):
            x = norm(pnow[r], g_in[w : w + 1, :]).astype(BF16)
            here = jnp.sum(jnp.where(lanes == 2 * me + r, am, 0.0), axis=-1, keepdims=True)
            mask = am * here
            pt = dot_nt(wt[w], x)
            for side in range(2):
                at = side * 256
                val = jax.nn.sigmoid(pt[at + 128 : at + 256]) * pt[at : at + 128] * mask
                for j in range(2):
                    t32[pl.ds(side * 4 + r * 2 + j, 128, stride=8), :] = val[
                        :, j * 128 : (j + 1) * 128
                    ]
            tx[r] = x
        tsend[w] = t32[...].reshape(N, 8, 128).astype(BF16)
        trecv[w, me] = tsend[w, me]
        exchange(tsend.at[w], trecv.at[w], 6 + 2 * w)
        for r in range(2):
            tgate[r] = jax.nn.sigmoid(dot(tx[r], wgate[w]))
        received(tsend.at[w], trecv.at[w], 6 + 2 * w)
        t32[...] = trecv[w].astype(F32).reshape(N * 8, 128)
        sides = []
        for side in range(2):
            sides.append(
                jnp.concatenate(
                    [
                        jnp.concatenate(
                            [
                                t32[pl.ds(side * 4 + r * 2 + j, 128, stride=8), :]
                                for j in range(2)
                            ],
                            axis=1,
                        )
                        for r in range(2)
                    ],
                    axis=0,
                )
            )
        if w == 0:
            prod = dot_nt(sides[0].astype(BF16), sides[1].astype(BF16))
        else:
            prod = dot(sides[0].T.astype(BF16), sides[1].astype(BF16))
        for j in range(2):
            xn[j] = prod[:, j * 128 : (j + 1) * 128]
        for r in range(2):
            for j in range(2):
                rows = pl.ds(r * 128, 128) if w == 0 else pl.ds(r, 128, stride=2)
                p32[pl.ds(r * 2 + j, 128, stride=4), :] = xn[j, rows, :]
        psend[w] = p32[...].reshape(N, 4, 128).astype(BF16)
        precv[w, me] = psend[w, me]
        exchange(psend.at[w], precv.at[w], 7 + 2 * w)
        received(psend.at[w], precv.at[w], 7 + 2 * w)
        p32[...] = precv[w].astype(F32).reshape(N * 4, 128)
        for r in range(2):
            for j in range(2):
                pn = norm(p32[pl.ds(r * 2 + j, 128, stride=4), :], gmt[w], axis=0)
                update = dot(pn.T.astype(BF16), wout[w])
                rows = pl.ds(j, 128, stride=2) if w == 0 else pl.ds(j * 128, 128)
                new = pnow[r, rows, :] + update * tgate[r, rows, :]
                if w == 0:
                    pnow[r, rows, :] = new
                else:
                    pair_out[r, rows, :] = new

    for like, sem in sent:
        landed(like, ssem.at[sem])


def copied(a, b, a_out, b_out, sems):
    pltpu.make_async_copy(a, a_out, sems.at[0]).start()
    pltpu.make_async_copy(b, b_out, sems.at[1]).start()
    pltpu.make_async_copy(a, a_out, sems.at[0]).wait()
    pltpu.make_async_copy(b, b_out, sems.at[1]).wait()


SCRATCH = [
    ((BA, 128), BF16),
    ((BB, 128), BF16),
    ((BC, 128), BF16),
    ((2, N // 2, BA, 128), BF16),
    ((2, N // 2, BB, 128), BF16),
    ((2, N // 2, BC, 128), BF16),
    ((N * BA, 128), F32),
    ((N * BB, 128), F32),
    ((N * BC, 128), F32),
    ((2, S, HEADS * S), F32),
    ((2, S, CZ), BF16),
    ((2, S, 128), F32),
    ((2, 2, S, 128), F32),
    ((2, S, H), BF16),
    ((2, H, S), BF16),
    ((2, HEADS * S, H), BF16),
    ((2, S, HEADS * S), BF16),
    ((2, S, H), F32),
    ((N * 8, 128), F32),
    ((N, 8, 128), BF16),
    ((N, 8, 128), BF16),
    ((2, S, H), F32),
    ((S, S), F32),
    ((S, S), BF16),
    ((2, S, CZ), F32),
    ((2, 32, S), BF16),
    ((2, 32, S), BF16),
    ((LINE, 2, 32, S), BF16),
    ((2, PLANE, 32, S), BF16),
    ((2, 512, 128), F32),
    ((2, 512, S), BF16),
    ((128, 4096), BF16),
    ((4096, 512), BF16),
    ((LINE, 2, 32, 128), BF16),
    ((LINE, 2, 32, 128), BF16),
    ((2, 512, 128), BF16),
    ((2, CZ, CZ), F32),
    ((BA + BB + BC, 128), F32),
    ((N * 8, 128), F32),
    ((2, N, 8, 128), BF16),
    ((2, N, 8, 128), BF16),
    ((2, S, CZ), F32),
    ((N * 4, 128), F32),
    ((2, N, 4, 128), BF16),
    ((2, N, 4, 128), BF16),
    ((2, S, CZ), F32),
]


def shards(*args):
    args = [a.reshape(1, -1) if a.ndim == 1 else a for a in args]
    for n in (9, 15):
        args[n] = args[n].T
    anywhere = pl.BlockSpec(memory_space=pl.ANY)
    local = pl.BlockSpec(memory_space=pltpu.VMEM)
    results = (
        jax.ShapeDtypeStruct((S * 4, 128), F32),
        jax.ShapeDtypeStruct((2, S, CZ), F32),
    )
    flat, pair = pl.pallas_call(
        body,
        out_shape=tuple(pltpu.VMEM(a.shape, a.dtype) for a in results),
        in_specs=[anywhere] * N_IN,
        out_specs=(local, local),
        scratch_shapes=[pltpu.VMEM(a.shape, a.dtype) for a in args]
        + [pltpu.VMEM(shape, dtype) for shape, dtype in SCRATCH]
        + [pltpu.SemaphoreType.DMA((n,)) for n in (15, 15, N_IN)],
        compiler_params=pltpu.CompilerParams(
            collective_id=0, has_side_effects=True, vmem_limit_bytes=60 << 20
        ),
    )(*args)
    flat, pair = pl.pallas_call(
        copied,
        out_shape=results,
        in_specs=[local] * 2,
        out_specs=(anywhere, anywhere),
        scratch_shapes=[pltpu.SemaphoreType.DMA((2,))],
    )(*(pltpu.with_memory_space_constraint(a, pltpu.VMEM) for a in (flat, pair)))
    return flat.reshape(S, 2, 2, 128).transpose(0, 2, 1, 3).reshape(S, 2, H), pair


def solution(mesh):
    rows = P("dap", None, None)
    return jax.shard_map(
        shards,
        mesh=mesh,
        in_specs=(rows, rows, P("dap", None)) + (P(),) * 19,
        out_specs=(P(None, "dap", None), rows),
        check_vma=False,
    )
```
